32 devices in a mesh: row: 8 (over y, x, core), col: 4 (over z).
Axes of the slice: x: 2, y: 2, z: 4, core: 2. Of those that a mesh axis runs over, the one named last changes fastest.
Arguments:
- velocity: bfloat16 [2048, 8, 3, 2048], P(('row', 'col')), may hold values from -6 to 6
- deriv_x: bfloat16 [2048, 2048], replicated, may hold values from -0.125 to 0.125
- deriv_y: bfloat16 [8, 8], replicated, may hold values from -2 to 2
- deriv_z: bfloat16 [2048, 2048], replicated, may hold values from -0.125 to 0.125
- metric_x: float32 [2048], replicated, may hold values from 0.5 to 2
- metric_y: float32 [8], replicated, may hold values from 0.5 to 2
- metric_z: float32 [2048], replicated, may hold values from 0.5 to 2
- ib_target: bfloat16 [32, 128, 3, 128], P(('row', 'col')), may hold values from -6 to 6
- ib_owner: int32 [32, 128], P(('row', 'col')), may hold values from 0 to 31, as said below
- ib_block: int32 [32, 128], P(('row', 'col')), may hold values from 0 to 8191
- ib_count: int32 [32], P(('row', 'col')), may hold values from 64 to 128, as said below
Outputs:
- forced: float32 [2048, 8, 3, 2048], P(('row', 'col'))
The draws below stay inside these ranges and needn't reach their ends.
Inputs may be any that keep to these rules, and one draw needn't show every extreme that they name: `ib_owner`: at most 8 live slots of one device name one owner; on every device the first 8 slots name one owner common to all devices. Only the first ib_count[s] slots of device s are live.
All inputs are finite; a program needn't handle non-finite values.
Results may differ from the reference program's by a relative error of at most 0.0019.
Values may be sent and summed in bfloat16 or wider, within the bound.
No kernel may reach another device: no remote copies, remote signals or barrier semaphores. Data moves between devices by JAX's collectives and lax.ppermute only.
A program may use at most 256 MiB of HBM per device.

```python
import math
import jax
import jax.numpy as jnp

NX = 2048
NZ = 2048
NY = 8
BLOCK = 128
MOST = 8
CAP = 128
ZD = 64
BLOCKS = 8192
DEVICES = 32


def draw_ib_owner(key, part):
    first_key, second_key = jax.random.split(jax.random.fold_in(key, 11))
    hottest = jax.random.randint(first_key, (), 0, DEVICES)
    strides = 2 * jax.random.randint(second_key, (DEVICES, 1), 0, 4) + 1
    groups = (jnp.arange(CAP) // MOST)[None, :]
    return ((hottest + groups * strides) % DEVICES).astype(jnp.int32)


def draw_ib_count(key, part):
    first_key, second_key = jax.random.split(jax.random.fold_in(key, 23))
    counts = jax.random.randint(first_key, (DEVICES,), CAP // 2, CAP + 1)
    chosen = jax.random.randint(second_key, (), 0, DEVICES)
    index = jnp.arange(DEVICES)
    counts = jnp.where(index == chosen, CAP, counts)
    counts = jnp.where(index == (chosen + 1) % DEVICES, CAP // 2, counts)
    return counts.astype(jnp.int32)


def with_ends(result, rng, least, top_value):
    shape = result.shape
    place = [jax.random.randint(jax.random.fold_in(rng, axis), (), 0, shape[axis]) for axis in range(len(shape))]
    result = result.at[tuple(place)].set(least)
    longest = shape.index(max(shape))
    place[longest] = (place[longest] + 1) % shape[longest]
    return result.at[tuple(place)].set(top_value)


def block_levels(rng, shape, cuts, smallest, largest):
    def one(position, shards_of):
        draws = jax.random.uniform(jax.random.fold_in(jax.random.fold_in(rng, 6), position), (shards_of,), jnp.float32, smallest / len(cuts), largest / len(cuts))
        return jnp.repeat(jnp.exp(draws), shape[position] // shards_of).reshape((-1,) + (1,) * (len(shape) - position - 1))

    level = one(*cuts[0])
    for cut in cuts[1:]:
        level = level * one(*cut)
    return level


def centred(stream_key, extent, scale, most, pieces=(), held_as=jnp.bfloat16):
    result = scale * jax.random.normal(stream_key, extent, jnp.float32)
    if pieces:
        result = result * block_levels(stream_key, extent, pieces, -0.22, 0.18)
    return jnp.clip(result, -most, most).astype(held_as)


def setup_inputs(seed: int = 0) -> dict:
    seeds = jax.random.split(jax.random.key(seed), 12)
    velocity = centred(seeds[0], (NZ, NY, 3, NX), 1.0, 6.0, ((0, 32),))
    deriv_x = centred(seeds[1], (NX, NX), NX ** -0.5, 0.125)
    deriv_y = centred(seeds[2], (NY, NY), NY ** -0.5, 2.0)
    deriv_z = centred(seeds[3], (NZ, NZ), NZ ** -0.5, 0.125)
    metric_x = jnp.clip(jnp.exp(jax.random.uniform(seeds[4], (NX,), jnp.float32, math.log(0.5), math.log(2.0))), 0.5, 2.0)
    metric_y = jnp.clip(jnp.exp(jax.random.uniform(seeds[5], (NY,), jnp.float32, math.log(0.5), math.log(2.0))), 0.5, 2.0)
    metric_z = jnp.clip(jnp.exp(jax.random.uniform(seeds[6], (NZ,), jnp.float32, math.log(0.5), math.log(2.0))), 0.5, 2.0)
    ib_target = centred(seeds[7], (DEVICES, CAP, 3, BLOCK), 1.0, 6.0, ((0, 32),))
    ib_owner = draw_ib_owner(jax.random.fold_in(seeds[11], 71), 0)
    ib_block = with_ends(jax.random.randint(seeds[9], (DEVICES, CAP), 0, BLOCKS), jax.random.fold_in(seeds[9], 1), 0, BLOCKS - 1).astype(jnp.int32)
    ib_count = draw_ib_count(jax.random.fold_in(seeds[11], 71), 0)
    return dict(velocity=velocity, deriv_x=deriv_x, deriv_y=deriv_y, deriv_z=deriv_z, metric_x=metric_x, metric_y=metric_y, metric_z=metric_z, ib_target=ib_target, ib_owner=ib_owner, ib_block=ib_block, ib_count=ib_count)


viscosity = 0.4
time_step = 0.2


def reference(velocity, deriv_x, deriv_y, deriv_z, metric_x, metric_y, metric_z, ib_target, ib_owner, ib_block, ib_count):
    speeds = velocity.astype(jnp.float32)
    shape = velocity.shape
    line_rows = velocity.reshape(-1, NX)
    grad_x = (jnp.dot(line_rows, deriv_x.T, preferred_element_type=jnp.float32) * metric_x).astype(jnp.bfloat16)
    curv_x = (jnp.dot(grad_x, deriv_x.T, preferred_element_type=jnp.float32) * metric_x).reshape(shape)
    grad_x = grad_x.reshape(shape)
    weights_y = deriv_y.astype(jnp.float32)
    scale_y = metric_y[None, :, None, None]
    grad_y = (jnp.einsum("ij,zjcx->zicx", weights_y, speeds) * scale_y).astype(jnp.bfloat16)
    curv_y = jnp.einsum("ij,zjcx->zicx", weights_y, grad_y.astype(jnp.float32)) * scale_y
    depth_rows = velocity.reshape(NZ, -1)
    grad_z = (jnp.dot(deriv_z, depth_rows, preferred_element_type=jnp.float32) * metric_z[:, None]).astype(jnp.bfloat16)
    curv_z = (jnp.dot(deriv_z, grad_z, preferred_element_type=jnp.float32) * metric_z[:, None]).reshape(shape)
    grad_z = grad_z.reshape(shape)
    depth_term = (viscosity * curv_z - speeds[:, :, 2:3, :] * grad_z.astype(jnp.float32)).astype(jnp.bfloat16)
    tendency = -(speeds[:, :, 0:1, :] * grad_x.astype(jnp.float32) + speeds[:, :, 1:2, :] * grad_y.astype(jnp.float32))
    tendency = tendency + viscosity * (curv_x + curv_y) + depth_term.astype(jnp.float32)
    predicted = speeds + time_step * tendency
    xblocks = NX // BLOCK
    active = (jnp.arange(CAP)[None, :] < ib_count[:, None]).astype(jnp.float32)
    zrow_local = ib_block // (NY * xblocks)
    plane = (ib_block // xblocks) % NY
    xblock_index = ib_block % xblocks
    depth_row = ib_owner * ZD + zrow_local
    flat_index = ((depth_row * NY + plane) * xblocks + xblock_index).reshape(-1).astype(jnp.int32)
    weights = ib_target.astype(jnp.float32) * active[:, :, None, None]
    total_blocks = NZ * NY * xblocks
    pulled = jnp.zeros((total_blocks, 3, BLOCK), jnp.float32).at[flat_index].add(weights.reshape(-1, 3, BLOCK))
    counts = jnp.zeros((total_blocks,), jnp.float32).at[flat_index].add(active.reshape(-1))
    pulled = jnp.transpose(pulled.reshape(NZ, NY, xblocks, 3, BLOCK), (0, 1, 3, 2, 4))
    counts = counts.reshape(NZ, NY, 1, xblocks, 1)
    fields = predicted.reshape(NZ, NY, 3, xblocks, BLOCK)
    forced = (fields + pulled) / (1.0 + counts)
    return forced.reshape(shape)
```

```python
import functools

import jax
import jax.numpy as jnp
import numpy as np
from jax import lax
from jax.experimental import pallas as pl
from jax.experimental.pallas import tpu as pltpu
from jax.sharding import PartitionSpec as P

BLOCK = 128
MOST = 8
GROUP = 16
CHUNKS = 4

viscosity = 0.4
time_step = 0.2

F32 = jnp.float32
BF16 = jnp.bfloat16
AXES = ("row", "col")


def mm(a, b):
    return lax.dot_general(a, b, (((1,), (0,)), ((), ())), preferred_element_type=F32)


def mm_nt(a, b):
    return lax.dot_general(a, b, (((1,), (1,)), ((), ())), preferred_element_type=F32)


def pack_order(planes, comps):
    rows = GROUP * planes * comps
    table = np.zeros((rows, rows), np.float32)
    for y in range(planes):
        for c in range(comps):
            for z in range(GROUP):
                table[(y * comps + c) * GROUP + z, (z * comps + c) * planes + y] = 1
    return table


def unpack_order(planes, group):
    rows = group * planes
    table = np.zeros((rows, rows), np.float32)
    for y in range(planes):
        for z in range(group):
            table[z * planes + y, y * group + z] = 1
    return table


def pack_body(planes, comps, wide, order_ref, v_ref, o_ref):
    lanes = v_ref.shape[1]
    rows = order_ref.shape[0]
    for g in range(v_ref.shape[0] // rows):
        moved = mm(order_ref[...], v_ref[g * rows : (g + 1) * rows, :]).astype(BF16)
        for xg in range(lanes // wide):
            for y in range(planes):
                for c in range(comps):
                    at = (y * comps + c) * GROUP
                    o_ref[xg * planes + y, g * GROUP : (g + 1) * GROUP, c * wide : (c + 1) * wide] = moved[
                        at : at + GROUP, xg * wide : (xg + 1) * wide
                    ]


def pack(lines, order, chunk, chunks, planes, comps, devices, slab):
    columns = lines.shape[1]
    width = columns // chunks
    wide = width * planes // devices
    step = max(wide, 256)
    steps = width // step
    return pl.pallas_call(
        functools.partial(pack_body, planes, comps, wide),
        out_shape=jax.ShapeDtypeStruct((devices, slab, comps * wide), BF16),
        grid=(steps,),
        in_specs=[
            pl.BlockSpec(order.shape, lambda i: (0, 0)),
            pl.BlockSpec((lines.shape[0], step), lambda i: (0, chunk * steps + i)),
        ],
        out_specs=pl.BlockSpec((step // wide * planes, slab, comps * wide), lambda i: (i, 0, 0)),
        compiler_params=pltpu.CompilerParams(vmem_limit_bytes=48 << 20),
        cost_estimate=pl.CostEstimate(
            flops=2 * lines.shape[0] * order.shape[0] * width,
            bytes_accessed=4 * lines.shape[0] * width,
            transcendentals=0,
        ),
        name="pack",
    )(order, lines)


def depth_body(wide, block, x_ref, d_ref, m_ref, o_ref, g_ref):
    phase = pl.program_id(0)
    at = pl.multiple_of(pl.program_id(1) * block, block)
    spot = pl.ds(at, block)

    @pl.when(phase == 0)
    def _():
        g_ref[spot, :] = (mm(d_ref[...], x_ref[...]) * m_ref[spot, :]).astype(BF16)

    @pl.when(phase == 1)
    def _():
        curv = mm(d_ref[...], g_ref[...]) * m_ref[spot, :]
        grad = g_ref[spot, :].astype(F32)
        upward = x_ref[spot, 2 * wide : 3 * wide].astype(F32)
        for c in range(3):
            part = slice(c * wide, (c + 1) * wide)
            o_ref[:, part] = (viscosity * curv[:, part] - upward * grad[:, part]).astype(BF16)


def depth(x, deriv_z, metric_z):
    height, cols = x.shape
    block = min(512, height)
    return pl.pallas_call(
        functools.partial(depth_body, cols // 3, block),
        out_shape=jax.ShapeDtypeStruct(x.shape, BF16),
        grid=(2, height // block),
        in_specs=[
            pl.BlockSpec(x.shape, lambda p, i: (0, 0)),
            pl.BlockSpec((block, height), lambda p, i: (i, 0)),
            pl.BlockSpec((height, 1), lambda p, i: (0, 0)),
        ],
        out_specs=pl.BlockSpec((block, cols), lambda p, i: (i * p, 0)),
        scratch_shapes=[pltpu.VMEM(x.shape, BF16)],
        compiler_params=pltpu.CompilerParams(vmem_limit_bytes=48 << 20),
        cost_estimate=pl.CostEstimate(
            flops=4 * height * height * cols,
            bytes_accessed=4 * height * height + 4 * height * cols,
            transcendentals=0,
        ),
        name="depth",
    )(x, deriv_z, metric_z)


def marker_body(capacity, count_ref, owner_row, owner_col, block_col, t_ref, o_ref):
    count = count_ref[0]
    earlier = lax.broadcasted_iota(jnp.int32, (capacity, capacity), 0)
    later = lax.broadcasted_iota(jnp.int32, (capacity, capacity), 1)
    same = (owner_col[...] == owner_row[...]) & (earlier < later)
    position = jnp.sum(same.astype(jnp.int32), axis=0, keepdims=True)
    slot = lax.broadcasted_iota(jnp.int32, (1, capacity), 1)
    places = o_ref.shape[0]
    slotted = jnp.where(slot < count, owner_row[...] * MOST + position, places)
    placing = (lax.broadcasted_iota(jnp.int32, (places, capacity), 0) == slotted).astype(F32).astype(BF16)
    for c in range(3):
        o_ref[:, c * BLOCK : (c + 1) * BLOCK] = mm(placing, t_ref[c]).astype(BF16)
    lane = lax.broadcasted_iota(jnp.int32, (capacity, BLOCK), 1)
    high = block_col[...] // 128
    low = block_col[...] - high * 128
    label = jnp.where(lane == 0, high, jnp.where(lane == 1, low, jnp.where(lane == 2, 1, 0)))
    o_ref[:, 3 * BLOCK :] = mm(placing, label.astype(F32).astype(BF16)).astype(BF16)


def markers(ib_target, ib_owner, ib_block, ib_count, devices):
    capacity = ib_owner.shape[1]
    return pl.pallas_call(
        functools.partial(marker_body, capacity),
        out_shape=jax.ShapeDtypeStruct((devices * MOST, 4 * BLOCK), BF16),
        in_specs=[pl.BlockSpec(memory_space=pltpu.SMEM)] + [pl.BlockSpec(memory_space=pltpu.VMEM)] * 4,
        out_specs=pl.BlockSpec(memory_space=pltpu.VMEM),
        compiler_params=pltpu.CompilerParams(vmem_limit_bytes=32 << 20),
        cost_estimate=pl.CostEstimate(flops=10**8, bytes_accessed=10**6, transcendentals=0),
        name="markers",
    )(
        ib_count,
        ib_owner,
        ib_owner.reshape(capacity, 1),
        ib_block.reshape(capacity, 1),
        jnp.transpose(ib_target[0], (1, 0, 2)),
    )


def near_body(planes, comps, v_ref, dx_ref, dy_ref, mx_ref, my_ref, got_ref, p_ref, inv_ref, g_ref, s_ref):
    rows, columns = v_ref.shape
    group = rows // (planes * comps)
    lines = group * planes
    part = 512
    first = pl.program_id(0) * lines
    xblocks = columns // BLOCK
    slots = got_ref.shape[0]
    lane = lax.broadcasted_iota(jnp.int32, (8, BLOCK), 1)
    pick = jnp.where(lane == 0, 128.0, jnp.where(lane < 3, 1.0, 0.0)).astype(BF16)
    label = mm_nt(pick, got_ref[:, 3 * BLOCK :])[0:1, :].astype(jnp.int32)
    s_ref[:, : 3 * BLOCK] = got_ref[:, : 3 * BLOCK]
    s_ref[:, 3 * BLOCK :] = jnp.ones((slots, BLOCK), BF16)
    line = (first + lax.broadcasted_iota(jnp.int32, (lines, slots), 0)) * xblocks + 1
    for j in range(columns // part):
        span = slice(j * part, (j + 1) * part)
        g_ref[:, span] = (mm_nt(v_ref[...], dx_ref[span, :]) * mx_ref[:, span]).astype(BF16)
    for j in range(columns // part):
        span = slice(j * part, (j + 1) * part)
        curv = mm_nt(g_ref[...], dx_ref[span, :]) * mx_ref[:, span]
        vel = v_ref[:, span]
        grad_y = (mm(dy_ref[...], vel) * my_ref[...]).astype(BF16)
        curv = curv + mm(dy_ref[...], grad_y) * my_ref[...]
        shape = (group, comps, planes, part)
        vel = vel.astype(F32).reshape(shape)
        grad_y = grad_y.astype(F32).reshape(shape)
        grad_x = g_ref[:, span].astype(F32).reshape(shape)
        curv = curv.reshape(shape)
        tendency = viscosity * curv - (vel[:, 0:1] * grad_x + vel[:, 1:2] * grad_y)
        near = vel + time_step * tendency
        for b in range(part // BLOCK):
            chosen = (line + (j * (part // BLOCK) + b) == label).astype(F32).astype(BF16)
            share = mm(chosen, s_ref[...])
            inverse = (1.0 / (1.0 + share[:, 3 * BLOCK :])).reshape(group, planes, BLOCK)
            cells = slice(b * BLOCK, (b + 1) * BLOCK)
            place = slice(j * part + b * BLOCK, j * part + (b + 1) * BLOCK)
            inv_ref[:, :, place] = inverse
            for c in range(comps):
                pulled = share[:, c * BLOCK : (c + 1) * BLOCK].reshape(group, planes, BLOCK)
                p_ref[:, c, :, place] = (near[:, c, :, cells] + pulled) * inverse


def near(lines, deriv_x, band_y, metric_x, metric_rows, got, planes, comps, slab):
    total, columns = lines.shape
    rows = GROUP * planes * comps
    return pl.pallas_call(
        functools.partial(near_body, planes, comps),
        out_shape=(
            jax.ShapeDtypeStruct((slab, comps, planes, columns), F32),
            jax.ShapeDtypeStruct((slab, planes, columns), F32),
        ),
        grid=(total // rows,),
        in_specs=[
            pl.BlockSpec((rows, columns), lambda i: (i, 0)),
            pl.BlockSpec(deriv_x.shape, lambda i: (0, 0), pipeline_mode=pl.Buffered(1)),
            pl.BlockSpec(band_y.shape, lambda i: (0, 0)),
            pl.BlockSpec((1, columns), lambda i: (0, 0)),
            pl.BlockSpec((rows, 1), lambda i: (0, 0)),
            pl.BlockSpec(got.shape, lambda i: (0, 0)),
        ],
        out_specs=(
            pl.BlockSpec((GROUP, comps, planes, columns), lambda i: (i, 0, 0, 0)),
            pl.BlockSpec((GROUP, planes, columns), lambda i: (i, 0, 0)),
        ),
        scratch_shapes=[pltpu.VMEM((rows, columns), BF16), pltpu.VMEM(got.shape, BF16)],
        compiler_params=pltpu.CompilerParams(vmem_limit_bytes=56 << 20),
        cost_estimate=pl.CostEstimate(
            flops=4 * total * columns * columns,
            bytes_accessed=6 * total * columns + 2 * columns * columns,
            transcendentals=0,
        ),
        name="near",
    )(lines, deriv_x, band_y, metric_x, metric_rows, got)


def last_body(planes, comps, wide, group, order_ref, r_ref, inv_ref, p_ref, o_ref):
    slab = p_ref.shape[0]
    for xg in range(r_ref.shape[0] // planes):
        for g in range(slab // group):
            some = slice(g * group, (g + 1) * group)
            taken = r_ref[xg * planes : (xg + 1) * planes, some, :].reshape(planes * group, comps * wide)
            moved = mm(order_ref[...], taken) * time_step
            cells = slice(xg * wide, (xg + 1) * wide)
            inverse = inv_ref[some, :, cells]
            for c in range(comps):
                term = moved[:, c * wide : (c + 1) * wide].reshape(group, planes, wide)
                o_ref[some, c, :, cells] = p_ref[some, c, :, cells] + term * inverse


def last(field, returned, inverse, order, chunk, chunks, planes, comps, devices, slab, group):
    columns = field.shape[-1]
    width = columns // chunks
    wide = width * planes // devices
    step = wide
    steps = width // step
    spec = pl.BlockSpec((slab, comps, planes, step), lambda i: (0, 0, 0, chunk * steps + i))
    return pl.pallas_call(
        functools.partial(last_body, planes, comps, wide, group),
        out_shape=jax.ShapeDtypeStruct(field.shape, F32),
        grid=(steps,),
        in_specs=[
            pl.BlockSpec(order.shape, lambda i: (0, 0)),
            pl.BlockSpec((step // wide * planes, slab, comps * wide), lambda i: (i, 0, 0)),
            pl.BlockSpec((slab, planes, step), lambda i: (0, 0, chunk * steps + i)),
            spec,
        ],
        out_specs=spec,
        input_output_aliases={3: 0},
        compiler_params=pltpu.CompilerParams(vmem_limit_bytes=48 << 20),
        cost_estimate=pl.CostEstimate(
            flops=2 * slab * comps * planes * width * 256,
            bytes_accessed=12 * slab * comps * planes * width,
            transcendentals=0,
        ),
        name="last",
    )(order, returned, inverse, field)


def exchange(x):
    return lax.all_to_all(x, AXES, split_axis=0, concat_axis=0, tiled=True)


def local(
    velocity,
    deriv_x,
    deriv_y,
    deriv_z,
    metric_x,
    metric_y,
    metric_z,
    ib_target,
    ib_owner,
    ib_block,
    ib_count,
):
    slab, planes, comps, columns = velocity.shape
    devices = lax.axis_size("row") * lax.axis_size("col")
    pairs = planes * (columns // BLOCK) // devices
    chunks = min(CHUNKS, pairs)
    group = min(32, slab)
    lines = jnp.transpose(velocity, (0, 2, 1, 3)).reshape(slab * comps * planes, columns)
    order = jnp.asarray(pack_order(planes, comps), BF16)
    back = jnp.asarray(unpack_order(planes, group), BF16)
    arrived = []
    for k in range(chunks):
        arrived.append(exchange(pack(lines, order, k, chunks, planes, comps, devices, slab)))
        if k == 0:
            marked = markers(ib_target, ib_owner, ib_block, ib_count, devices)
            got = exchange(marked.reshape(devices, MOST, 4 * BLOCK)).reshape(devices * MOST, 4 * BLOCK)
    returned = []
    for k in range(chunks):
        x = arrived[k]
        result = depth(x.reshape(devices * slab, x.shape[2]), deriv_z, metric_z[:, None])
        returned.append(exchange(result.reshape(x.shape)))
    rows = GROUP * planes * comps
    band_y = jnp.kron(jnp.eye(GROUP * comps, dtype=F32), deriv_y.astype(F32)).astype(BF16)
    metric_rows = jnp.tile(metric_y, GROUP * comps)[:, None]
    field, inverse = near(
        lines, deriv_x, band_y, metric_x[None, :], metric_rows, got, planes, comps, slab
    )
    for k in range(chunks):
        field = last(
            field, returned[k], inverse, back, k, chunks, planes, comps, devices, slab, group
        )
    return jnp.transpose(field, (0, 2, 1, 3))


def solution(mesh):
    in_specs = (
        P(AXES, None, None, None),
        P(),
        P(),
        P(),
        P(),
        P(),
        P(),
        P(AXES, None, None, None),
        P(AXES, None),
        P(AXES, None),
        P(AXES),
    )
    out_specs = P(AXES, None, None, None)
    return jax.shard_map(local, mesh=mesh, in_specs=in_specs, out_specs=out_specs, check_vma=False)
```

```python
import functools

import jax
import jax.numpy as jnp
import numpy as np
from jax import lax
from jax.experimental import pallas as pl
from jax.experimental.pallas import tpu as pltpu
from jax.sharding import PartitionSpec as P

BLOCK = 128
MOST = 8
GROUP = 16
QUARTERS = 4
VMEM = 60 << 20
SHORT = 1
LONG = 10**12

viscosity = 0.4
time_step = 0.2

F32 = jnp.float32
BF16 = jnp.bfloat16
AXES = ("row", "col")


def cost(flops):
    return pl.CostEstimate(flops=flops, bytes_accessed=1, transcendentals=0)


def mm(a, b):
    return lax.dot_general(a, b, (((1,), (0,)), ((), ())), preferred_element_type=F32)


def mm_nt(a, b):
    return lax.dot_general(a, b, (((1,), (1,)), ((), ())), preferred_element_type=F32)


def pack_order(planes, comps):
    rows = GROUP * planes * comps
    table = np.zeros((rows, rows), np.float32)
    for y in range(planes):
        for c in range(comps):
            for z in range(GROUP):
                table[(y * comps + c) * GROUP + z, (z * comps + c) * planes + y] = 1
    return table


def unpack_order(planes, group):
    rows = group * planes
    table = np.zeros((rows, rows), np.float32)
    for y in range(planes):
        for z in range(group):
            table[z * planes + y, y * group + z] = 1
    return table


def place_rows(o_ref, moved, planes, comps, wide, at_rows, spot):
    for y in range(planes):
        for c in range(comps):
            at = (y * comps + c) * GROUP
            o_ref[y, at_rows, c * wide : (c + 1) * wide] = moved[at : at + GROUP, spot]


def pack_body(planes, comps, wide, order_ref, v_ref, o_ref):
    lanes = v_ref.shape[1]
    rows = order_ref.shape[0]
    for g in range(v_ref.shape[0] // rows):
        moved = mm(order_ref[...], v_ref[g * rows : (g + 1) * rows, :]).astype(BF16)
        for xg in range(lanes // wide):
            place_rows(
                o_ref.at[:, xg],
                moved,
                planes,
                comps,
                wide,
                slice(g * GROUP, (g + 1) * GROUP),
                slice(xg * wide, (xg + 1) * wide),
            )


def pack(lines, order, count, planes, comps, groups, slab):
    step = 2 * BLOCK
    steps = groups // 2
    return pl.pallas_call(
        functools.partial(pack_body, planes, comps, BLOCK),
        out_shape=jax.ShapeDtypeStruct((planes, groups, count * slab, comps * BLOCK), BF16),
        grid=(count, steps),
        in_specs=[
            pl.BlockSpec(order.shape, lambda q, i: (0, 0)),
            pl.BlockSpec((lines.shape[0], step), lambda q, i: (0, q * steps + i)),
        ],
        out_specs=pl.BlockSpec((planes, 2, slab, comps * BLOCK), lambda q, i: (0, i, q, 0)),
        compiler_params=pltpu.CompilerParams(vmem_limit_bytes=VMEM),
        cost_estimate=cost(SHORT),
        name="pack",
    )(order, lines)


def pack_apart_body(planes, comps, wide, ways, count, steps, me_ref, order_ref, *rest):
    v_refs, o_refs = rest[:ways], rest[ways + count :]
    step = pl.program_id(0)

    @pl.when(step < steps)
    def _():
        whole = jnp.concatenate([v_ref[...] for v_ref in v_refs], axis=1)
        moved = mm(order_ref[...], whole).astype(BF16)
        for k in range(ways):
            place_rows(o_refs[k], moved, planes, comps, wide, slice(None), slice(k * wide, (k + 1) * wide))

    if count >= ways:
        m_refs = rest[ways : 2 * ways]

        @pl.when(step == steps)
        def _():
            for k in range(ways):
                o_refs[k][:, :MOST, :] = m_refs[k][:, 0, :, : comps * BLOCK]
                o_refs[k][:, MOST:, :BLOCK] = m_refs[k][:, 0, :, comps * BLOCK :]
                o_refs[k][:, MOST:, BLOCK:] = jnp.zeros((planes, MOST, (comps - 1) * BLOCK), BF16)


def pack_apart(lines, order, me, chunk, planes, comps, ways, slab, after, marked=None):
    total = lines.shape[0]
    wide = BLOCK
    rows = order.shape[0]
    steps = total // rows
    more = 0 if marked is None else 1
    given = () if marked is None else (marked,) * ways
    return pl.pallas_call(
        functools.partial(pack_apart_body, planes, comps, wide, ways, len(given) + len(after), steps),
        out_shape=(jax.ShapeDtypeStruct((planes, slab + more * GROUP, comps * wide), BF16),) * ways,
        grid_spec=pltpu.PrefetchScalarGridSpec(
            num_scalar_prefetch=1,
            grid=(steps + more,),
            in_specs=[pl.BlockSpec(order.shape, lambda i, m: (0, 0))]
            + [
                pl.BlockSpec(
                    (rows, wide), lambda i, m, k=k: (jnp.minimum(i, steps - 1), chunk * ways + (m[0] ^ k))
                )
                for k in range(ways)
            ]
            + [
                pl.BlockSpec((planes, 1, MOST, (comps + 1) * BLOCK), lambda i, m, k=k: (0, m[0] ^ k, 0, 0))
                for k in range(ways if more else 0)
            ]
            + [pl.BlockSpec(memory_space=pltpu.HBM)] * len(after),
            out_specs=(pl.BlockSpec((planes, GROUP, comps * wide), lambda i, m: (0, i, 0)),) * ways,
        ),
        compiler_params=pltpu.CompilerParams(vmem_limit_bytes=VMEM),
        cost_estimate=cost(SHORT),
        name="pack_apart",
    )(me, order, *([lines] * ways), *given, *after)


def join_body(ways, *refs):
    o_ref = refs[-1]
    for k in range(ways):
        o_ref[:, k] = refs[k][...]


def join(pieces, after):
    ways = len(pieces)
    planes, height, cols = pieces[0].shape
    half = planes // 2
    return pl.pallas_call(
        functools.partial(join_body, ways),
        out_shape=jax.ShapeDtypeStruct((planes, ways, height, cols), BF16),
        grid=(2,),
        in_specs=[pl.BlockSpec((half, height, cols), lambda i: (i, 0, 0))] * ways
        + [pl.BlockSpec(memory_space=pltpu.HBM)] * len(after),
        out_specs=pl.BlockSpec((half, ways, height, cols), lambda i: (i, 0, 0, 0)),
        compiler_params=pltpu.CompilerParams(vmem_limit_bytes=VMEM),
        cost_estimate=cost(LONG),
        name="join",
    )(*pieces, *after)


def split_body(ways, count, x_ref, *rest):
    for k in range(1, ways):
        rest[count + k - 1][...] = x_ref[:, k]


def split(x, quarter, slab, after):
    planes, ways, _, cols = x.shape
    half = planes // 2
    return pl.pallas_call(
        functools.partial(split_body, ways, len(after)),
        out_shape=(jax.ShapeDtypeStruct((planes, slab, cols), BF16),) * (ways - 1),
        grid=(2,),
        in_specs=[pl.BlockSpec((half, ways, slab, cols), lambda i: (i, 0, quarter, 0))]
        + [pl.BlockSpec(memory_space=pltpu.HBM)] * len(after),
        out_specs=(pl.BlockSpec((half, slab, cols), lambda i: (i, 0, 0)),) * (ways - 1),
        compiler_params=pltpu.CompilerParams(vmem_limit_bytes=VMEM),
        cost_estimate=cost(SHORT),
        name="split",
    )(x, *after)


def depth_body(count, slab, block, extra, near_in, near_out, me_ref, x_ref, d_ref, m_ref, *rest):
    o_ref, s_ref, g_ref = rest[extra:]
    tall, ways, _, cols = x_ref.shape
    wide = cols // 3
    phase = pl.program_id(0)
    step = pl.program_id(1)
    spot = pl.ds(pl.multiple_of(step * block, block), block)
    me = me_ref[0]

    @pl.when((phase == 0) & (step == 0))
    def _():
        for r in range(tall):
            for k in range(ways):
                to = pl.multiple_of((r * ways + (me ^ k if near_in else k)) * slab, slab)
                for q in range(count):
                    s_ref[pl.ds(to, slab), q * cols : (q + 1) * cols] = x_ref[r, k, q * slab : (q + 1) * slab]

    @pl.when(phase == 0)
    def _():
        g_ref[spot, :] = (mm(d_ref[...], s_ref[...]) * m_ref[spot, :]).astype(BF16)

    @pl.when(phase == 1)
    def _():
        curv = mm(d_ref[...], g_ref[...]) * m_ref[spot, :]
        grad = g_ref[spot, :].astype(F32)
        each = block // slab
        for q in range(count):
            upward = s_ref[spot, q * cols + 2 * wide : q * cols + 3 * wide].astype(F32)
            for c in range(3):
                part = slice(q * cols + c * wide, q * cols + (c + 1) * wide)
                term = (viscosity * curv[:, part] - upward * grad[:, part]).astype(BF16)
                for n in range(each):
                    r = step * (each // ways) + n // ways
                    k = me ^ (n % ways) if near_out else n % ways
                    o_ref[r, k, q * slab : (q + 1) * slab, c * wide : (c + 1) * wide] = term[
                        n * slab : (n + 1) * slab, :
                    ]


def depth(x, me, deriv_z, metric_z, count, slab, near_in, near_out, after, place=0, total=None, held=()):
    tall, ways, _, cols = x.shape
    shape = (tall, ways, count * slab, cols)
    extra = tuple(held) + tuple(after)
    height = deriv_z.shape[0]
    block = 512
    return pl.pallas_call(
        functools.partial(depth_body, count, slab, block, len(extra), near_in, near_out),
        out_shape=jax.ShapeDtypeStruct((tall, ways, (total or count) * slab, cols), BF16),
        grid_spec=pltpu.PrefetchScalarGridSpec(
            num_scalar_prefetch=1,
            grid=(2, height // block),
            in_specs=[
                pl.BlockSpec(shape, lambda p, i, m: (0, 0, 0, 0)),
                pl.BlockSpec((block, height), lambda p, i, m: (i, 0)),
                pl.BlockSpec((height, 1), lambda p, i, m: (0, 0)),
            ]
            + [pl.BlockSpec(memory_space=pltpu.HBM)] * len(extra),
            out_specs=pl.BlockSpec(shape, lambda p, i, m: (0, 0, place, 0)),
            scratch_shapes=[pltpu.VMEM((height, count * cols), BF16), pltpu.VMEM((height, count * cols), BF16)],
        ),
        input_output_aliases={4: 0} if held else {},
        compiler_params=pltpu.CompilerParams(vmem_limit_bytes=VMEM),
        cost_estimate=cost(SHORT),
        name="depth",
    )(me, x, deriv_z, metric_z, *extra)


def marker_body(capacity, count_ref, owner_row, owner_col, block_col, t_ref, o_ref):
    count = count_ref[0]
    earlier = lax.broadcasted_iota(jnp.int32, (capacity, capacity), 0)
    later = lax.broadcasted_iota(jnp.int32, (capacity, capacity), 1)
    same = (owner_col[...] == owner_row[...]) & (earlier < later)
    position = jnp.sum(same.astype(jnp.int32), axis=0, keepdims=True)
    slot = lax.broadcasted_iota(jnp.int32, (1, capacity), 1)
    places = o_ref.shape[0]
    slotted = jnp.where(slot < count, owner_row[...] * MOST + position, places)
    placing = (lax.broadcasted_iota(jnp.int32, (places, capacity), 0) == slotted).astype(F32).astype(BF16)
    for c in range(3):
        o_ref[:, c * BLOCK : (c + 1) * BLOCK] = mm(placing, t_ref[c]).astype(BF16)
    lane = lax.broadcasted_iota(jnp.int32, (capacity, BLOCK), 1)
    high = block_col[...] // 128
    low = block_col[...] - high * 128
    label = jnp.where(lane == 0, high, jnp.where(lane == 1, low, jnp.where(lane == 2, 1, 0)))
    o_ref[:, 3 * BLOCK :] = mm(placing, label.astype(F32).astype(BF16)).astype(BF16)


def markers(ib_target, ib_owner, ib_block, ib_count, devices):
    capacity = ib_owner.shape[1]
    return pl.pallas_call(
        functools.partial(marker_body, capacity),
        out_shape=jax.ShapeDtypeStruct((devices * MOST, 4 * BLOCK), BF16),
        in_specs=[pl.BlockSpec(memory_space=pltpu.SMEM)] + [pl.BlockSpec(memory_space=pltpu.VMEM)] * 4,
        out_specs=pl.BlockSpec(memory_space=pltpu.VMEM),
        compiler_params=pltpu.CompilerParams(vmem_limit_bytes=VMEM),
        cost_estimate=cost(SHORT),
        name="markers",
    )(
        ib_count,
        ib_owner,
        ib_owner.reshape(capacity, 1),
        ib_block.reshape(capacity, 1),
        jnp.transpose(ib_target[0], (1, 0, 2)),
    )


def near_body(planes, comps, extra, v_ref, dx_ref, dy_ref, mx_ref, my_ref, *rest):
    p_ref, g_ref, band_ref, scale_ref = rest[extra:]
    rows, columns = v_ref.shape
    group = rows // (planes * comps)
    part = 512

    @pl.when(pl.program_id(0) == 0)
    def _():
        row = lax.broadcasted_iota(jnp.int32, (rows, planes), 0) % planes
        take = (row == lax.broadcasted_iota(jnp.int32, (rows, planes), 1)).astype(F32)
        scale_ref[...] = jnp.sum(take * my_ref[...], axis=1, keepdims=True)
        take = take.astype(BF16)
        spread = mm_nt(mm(take, dy_ref[...]).astype(BF16), take)
        one = lax.broadcasted_iota(jnp.int32, (rows, rows), 0) // planes
        other = lax.broadcasted_iota(jnp.int32, (rows, rows), 1) // planes
        band_ref[...] = jnp.where(one == other, spread, 0.0).astype(BF16)

    for j in range(columns // part):
        span = slice(j * part, (j + 1) * part)
        g_ref[:, span] = (mm_nt(v_ref[...], dx_ref[span, :]) * mx_ref[:, span]).astype(BF16)
    for j in range(columns // part):
        span = slice(j * part, (j + 1) * part)
        curv = mm_nt(g_ref[...], dx_ref[span, :]) * mx_ref[:, span]
        vel = v_ref[:, span]
        grad_y = (mm(band_ref[...], vel) * scale_ref[...]).astype(BF16)
        curv = curv + mm(band_ref[...], grad_y) * scale_ref[...]
        shape = (group, comps, planes, part)
        vel = vel.astype(F32).reshape(shape)
        grad_y = grad_y.astype(F32).reshape(shape)
        grad_x = g_ref[:, span].astype(F32).reshape(shape)
        curv = curv.reshape(shape)
        tendency = viscosity * curv - (vel[:, 0:1] * grad_x + vel[:, 1:2] * grad_y)
        p_ref[:, :, :, span] = vel + time_step * tendency


def near(lines, deriv_x, deriv_y, metric_x, metric_y, planes, comps, slab, after):
    total, columns = lines.shape
    rows = GROUP * planes * comps
    return pl.pallas_call(
        functools.partial(near_body, planes, comps, len(after)),
        out_shape=jax.ShapeDtypeStruct((slab, comps, planes, columns), F32),
        grid=(total // rows,),
        in_specs=[
            pl.BlockSpec((rows, columns), lambda i: (i, 0)),
            pl.BlockSpec(deriv_x.shape, lambda i: (0, 0), pipeline_mode=pl.Buffered(1)),
            pl.BlockSpec(deriv_y.shape, lambda i: (0, 0)),
            pl.BlockSpec((1, columns), lambda i: (0, 0)),
            pl.BlockSpec((1, planes), lambda i: (0, 0)),
        ]
        + [pl.BlockSpec(memory_space=pltpu.HBM)] * len(after),
        out_specs=pl.BlockSpec((GROUP, comps, planes, columns), lambda i: (i, 0, 0, 0)),
        scratch_shapes=[
            pltpu.VMEM((rows, columns), BF16),
            pltpu.VMEM((rows, rows), BF16),
            pltpu.VMEM((rows, 1), F32),
        ],
        compiler_params=pltpu.CompilerParams(vmem_limit_bytes=VMEM),
        cost_estimate=cost(SHORT),
        name="near",
    )(lines, deriv_x, deriv_y, metric_x, metric_y, *after)


def ready_markers(got_ref, s_ref, l_ref):
    lane = lax.broadcasted_iota(jnp.int32, (8, BLOCK), 1)
    pick = jnp.where(lane == 0, 128.0, jnp.where(lane < 3, 1.0, 0.0)).astype(BF16)
    slots = s_ref.shape[0]
    if len(got_ref.shape) == 4:
        values = got_ref[:, :, :MOST, :]
        meta = got_ref[:, :, MOST:, :BLOCK]
    else:
        values = got_ref[:, :, : 3 * BLOCK]
        meta = got_ref[:, :, 3 * BLOCK :]
    meta = meta.astype(F32).reshape(slots, BLOCK).astype(BF16)
    l_ref[...] = mm_nt(pick, meta).astype(jnp.int32)
    s_ref[:, : 3 * BLOCK] = values.astype(F32).reshape(slots, 3 * BLOCK).astype(BF16)
    s_ref[:, 3 * BLOCK :] = jnp.ones((slots, BLOCK), BF16)


def markers_spec(got, slab):
    if got.ndim == 4:
        block = (got.shape[0], got.shape[1], GROUP, got.shape[3])
        return pl.BlockSpec(block, lambda *_: (0, 0, slab // GROUP, 0)), got.shape[0] * got.shape[1] * MOST
    return pl.BlockSpec(got.shape, lambda *_: (0, 0, 0)), got.shape[0] * MOST


def settle(order_ref, taken, s_ref, l_ref, p_ref, o_ref, comps, wide, group, xblocks, first, at):
    slab = p_ref.shape[0]
    planes = p_ref.shape[2]
    lines = group * planes
    slots = s_ref.shape[0]
    label = l_ref[0:1, :]
    for g in range(slab // group):
        some = slice(g * group, (g + 1) * group)
        moved = mm(order_ref[...], taken(some).reshape(lines, comps * wide)) * time_step
        line = (g * lines + lax.broadcasted_iota(jnp.int32, (lines, slots), 0)) * xblocks + 1
        for b in range(wide // BLOCK):
            chosen = (line + (first + b) == label).astype(F32).astype(BF16)
            share = mm(chosen, s_ref[...])
            inverse = 1.0 / (1.0 + share[:, 3 * BLOCK :])
            cells = slice(at + b * BLOCK, at + (b + 1) * BLOCK)
            for c in range(comps):
                term = moved[:, c * wide + b * BLOCK : c * wide + (b + 1) * BLOCK]
                total = p_ref[some, c, :, cells].reshape(lines, BLOCK) + term + share[:, c * BLOCK : (c + 1) * BLOCK]
                o_ref[some, c, :, cells] = (total * inverse).reshape(group, planes, BLOCK)


def last_body(planes, comps, group, xblocks, start, order_ref, r_ref, got_ref, p_ref, o_ref, s_ref, l_ref):
    pairs = r_ref.shape[1]
    step = pl.program_id(0) * pl.num_programs(1) + pl.program_id(1)

    @pl.when(step == 0)
    def _():
        ready_markers(got_ref, s_ref, l_ref)

    for xg in range(pairs):
        settle(
            order_ref,
            lambda some, xg=xg: r_ref[:, xg, some, :],
            s_ref,
            l_ref,
            p_ref,
            o_ref,
            comps,
            BLOCK,
            group,
            xblocks,
            start + step * pairs + xg,
            xg * BLOCK,
        )


def last(field, returned, got, order, first, count, group):
    slab, comps, planes, columns = field.shape
    groups = returned.shape[1]
    steps = groups // 2
    spec = pl.BlockSpec((slab, comps, planes, 2 * BLOCK), lambda q, i: (0, 0, 0, (first + q) * steps + i))
    got_spec, slots = markers_spec(got, slab)
    return pl.pallas_call(
        functools.partial(last_body, planes, comps, group, columns // BLOCK, first * groups),
        out_shape=jax.ShapeDtypeStruct(field.shape, F32),
        grid=(count, steps),
        in_specs=[
            pl.BlockSpec(order.shape, lambda q, i: (0, 0)),
            pl.BlockSpec((planes, 2, slab, comps * BLOCK), lambda q, i: (0, i, q, 0)),
            got_spec,
            spec,
        ],
        out_specs=spec,
        input_output_aliases={3: 0},
        scratch_shapes=[pltpu.VMEM((slots, 4 * BLOCK), BF16), pltpu.VMEM((8, slots), jnp.int32)],
        compiler_params=pltpu.CompilerParams(vmem_limit_bytes=VMEM),
        cost_estimate=cost(SHORT),
        name="last",
    )(order, returned, got, field)


def last_apart_body(comps, group, xblocks, start, ways, me_ref, order_ref, got_ref, own_ref, *rest):
    pieces, p_ref = rest[: ways - 1], rest[ways - 1]
    o_ref, s_ref, l_ref, t_ref = rest[-4:]
    step = pl.program_id(0)

    @pl.when(step == 0)
    def _():
        ready_markers(got_ref, s_ref, l_ref)
        t_ref[...] = own_ref[:, 0]

    for k in range(1, ways):

        @pl.when(step == k)
        def _(k=k):
            t_ref[...] = pieces[k - 1][...]

    settle(
        order_ref,
        lambda some: t_ref[:, some, :],
        s_ref,
        l_ref,
        p_ref,
        o_ref,
        comps,
        BLOCK,
        group,
        xblocks,
        start + (me_ref[0] ^ step),
        0,
    )


def last_apart(field, own, pieces, got, order, me, chunk, group, after):
    slab, comps, planes, columns = field.shape
    ways = own.shape[1]
    spec = pl.BlockSpec((slab, comps, planes, BLOCK), lambda i, m: (0, 0, 0, chunk * ways + (m[0] ^ i)))
    whole = pl.BlockSpec((planes, slab, comps * BLOCK), lambda i, m: (0, 0, 0))
    got_spec, slots = markers_spec(got, slab)
    return pl.pallas_call(
        functools.partial(last_apart_body, comps, group, columns // BLOCK, chunk * ways, ways),
        out_shape=jax.ShapeDtypeStruct(field.shape, F32),
        grid_spec=pltpu.PrefetchScalarGridSpec(
            num_scalar_prefetch=1,
            grid=(ways,),
            in_specs=[
                pl.BlockSpec(order.shape, lambda i, m: (0, 0)),
                got_spec,
                pl.BlockSpec((planes, 1, slab, comps * BLOCK), lambda i, m: (0, 0, chunk, 0)),
            ]
            + [whole] * (ways - 1)
            + [spec]
            + [pl.BlockSpec(memory_space=pltpu.HBM)] * len(after),
            out_specs=spec,
            scratch_shapes=[
                pltpu.VMEM((slots, 4 * BLOCK), BF16),
                pltpu.VMEM((8, slots), jnp.int32),
                pltpu.VMEM((planes, slab, comps * BLOCK), BF16),
            ],
        ),
        input_output_aliases={4 + ways - 1: 0},
        compiler_params=pltpu.CompilerParams(vmem_limit_bytes=VMEM),
        cost_estimate=cost(LONG),
        name="last_apart",
    )(me, order, got, own, *pieces, field, *after)


def come_body(count, *refs):
    refs[count][...] = jnp.zeros_like(refs[count])


def come(pieces):
    return pl.pallas_call(
        functools.partial(come_body, len(pieces)),
        out_shape=jax.ShapeDtypeStruct((8, BLOCK), F32),
        in_specs=[pl.BlockSpec(memory_space=pltpu.HBM)] * len(pieces),
        out_specs=pl.BlockSpec(memory_space=pltpu.VMEM),
        cost_estimate=cost(LONG),
        name="come",
    )(*pieces)


def across(pieces):
    ways = lax.axis_size("col")
    return tuple(
        lax.ppermute(piece, "col", [(c, c ^ k) for c in range(ways)]) for k, piece in enumerate(pieces, 1)
    )


def along(x):
    return lax.all_to_all(x, "row", split_axis=0, concat_axis=0, tiled=True)


def exchange(x):
    return lax.all_to_all(x, AXES, split_axis=0, concat_axis=0, tiled=True)


def local(
    velocity,
    deriv_x,
    deriv_y,
    deriv_z,
    metric_x,
    metric_y,
    metric_z,
    ib_target,
    ib_owner,
    ib_block,
    ib_count,
):
    slab, planes, comps, columns = velocity.shape
    row_count, ways = lax.axis_size("row"), lax.axis_size("col")
    devices = row_count * ways
    groups = devices // planes
    group = min(32, slab)
    chunks = columns // (groups * BLOCK)
    me = lax.axis_index("col").astype(jnp.int32).reshape(1)
    lines = jnp.transpose(velocity, (0, 2, 1, 3)).reshape(slab * comps * planes, columns)
    order = jnp.asarray(pack_order(planes, comps), BF16)
    back = jnp.asarray(unpack_order(planes, group), BF16)
    metric_col = metric_z[:, None]
    marked = markers(ib_target, ib_owner, ib_block, ib_count, devices)
    apart = row_count == planes and chunks == QUARTERS and slab == QUARTERS * GROUP
    at_once = 2 if apart else chunks
    first = pack(lines, order, at_once, planes, comps, groups, slab)
    block = (devices,) + first.shape[2:]
    arrived = exchange(first.reshape(block)).reshape((row_count, ways) + first.shape[2:])
    field = near(
        lines, deriv_x, deriv_y, metric_x[None, :], metric_y[None, :], planes, comps, slab, (first,)
    )

    def terms_of(x, near_in, near_out, after):
        return depth(x, me, deriv_z, metric_col, at_once, slab, near_in, near_out, after)

    if not apart:
        got = exchange(marked.reshape(devices, MOST, 4 * BLOCK))
        terms = terms_of(arrived, False, False, (field,))
        home = exchange(terms.reshape(block)).reshape(first.shape)
        field = last(field, home, got, back, 0, chunks, group)
        return jnp.transpose(field, (0, 2, 1, 3))

    def outward(k, after, marked=None):
        return pack_apart(lines, order, me, k, planes, comps, ways, slab, after, marked)

    sent3 = outward(3, (field,))
    sent2 = outward(2, (sent3[0],), marked.reshape(planes, ways, MOST, (comps + 1) * BLOCK))
    later2, later3 = lax.optimization_barrier((sent2[1:], sent3[1:], arrived))[:2]
    come2 = across(later2)
    come3 = across(later3)
    terms = terms_of(arrived, False, True, (sent2[0],))
    home = along(terms)
    joined2 = join((sent2[0],) + come2, (terms,))
    split0 = split(home, 0, slab, (joined2,))
    back0 = across(split0)
    split1 = split(home, 1, slab, (split0[0],))
    back1 = across(split1)
    got = full2 = along(joined2)
    joined3 = join((sent3[0],) + come3, (split1[0],))
    full3 = along(joined3)
    terms = depth(full2, me, deriv_z, metric_col, 1, slab, True, False, (joined3,), 0, 2)
    terms = depth(full3, me, deriv_z, metric_col, 1, slab, True, False, (come(back0),), 1, 2, (terms,))
    home_all = exchange(terms.reshape(block)).reshape(first.shape)
    field = last_apart(field, home, back0, got, back, me, 0, group, (terms,))
    field = last_apart(field, home, back1, got, back, me, 1, group, ())
    field = last(field, home_all, got, back, 2, 2, group)
    return jnp.transpose(field, (0, 2, 1, 3))


def solution(mesh):
    in_specs = (
        P(AXES, None, None, None),
        P(),
        P(),
        P(),
        P(),
        P(),
        P(),
        P(AXES, None, None, None),
        P(AXES, None),
        P(AXES, None),
        P(AXES),
    )
    out_specs = P(AXES, None, None, None)
    return jax.shard_map(local, mesh=mesh, in_specs=in_specs, out_specs=out_specs, check_vma=False)
```

```python
import functools

import jax
import jax.numpy as jnp
import numpy as np
from jax import lax
from jax.experimental import pallas as pl
from jax.experimental.pallas import tpu as pltpu
from jax.sharding import PartitionSpec as P

BLOCK = 128
MOST = 8
GROUP = 16
QUARTERS = 4
VMEM = 60 << 20
ROOM = 60 << 20
SHORT = 1
EARLY = 2
PACK = 4
LONG = 10**12

viscosity = 0.4
time_step = 0.2

F32 = jnp.float32
BF16 = jnp.bfloat16
AXES = ("row", "col")


def cost(flops):
    return pl.CostEstimate(flops=flops, bytes_accessed=1, transcendentals=0)


def mm(a, b):
    return lax.dot_general(a, b, (((1,), (0,)), ((), ())), preferred_element_type=F32)


def mm_nt(a, b):
    return lax.dot_general(a, b, (((1,), (1,)), ((), ())), preferred_element_type=F32)


def pack_order(planes, comps):
    rows = GROUP * planes * comps
    table = np.zeros((rows, rows), np.float32)
    for y in range(planes):
        for c in range(comps):
            for z in range(GROUP):
                table[(y * comps + c) * GROUP + z, (z * comps + c) * planes + y] = 1
    return table


def unpack_order(planes, group):
    rows = group * planes
    table = np.zeros((rows, rows), np.float32)
    for y in range(planes):
        for z in range(group):
            table[z * planes + y, y * group + z] = 1
    return table


def place_rows(o_ref, moved, planes, comps, wide, at_rows, spot):
    for y in range(planes):
        for c in range(comps):
            at = (y * comps + c) * GROUP
            o_ref[y, at_rows, c * wide : (c + 1) * wide] = moved[at : at + GROUP, spot]


def pack_body(planes, comps, wide, order_ref, v_ref, o_ref):
    lanes = v_ref.shape[1]
    rows = order_ref.shape[0]
    for g in range(v_ref.shape[0] // rows):
        moved = mm(order_ref[...], v_ref[g * rows : (g + 1) * rows, :]).astype(BF16)
        for xg in range(lanes // wide):
            place_rows(
                o_ref.at[:, xg],
                moved,
                planes,
                comps,
                wide,
                slice(g * GROUP, (g + 1) * GROUP),
                slice(xg * wide, (xg + 1) * wide),
            )


def pack(lines, order, count, planes, comps, groups, slab):
    many = PACK
    step = many * BLOCK
    steps = groups // many
    return pl.pallas_call(
        functools.partial(pack_body, planes, comps, BLOCK),
        out_shape=jax.ShapeDtypeStruct((planes, groups, count * slab, comps * BLOCK), BF16),
        grid=(count, steps),
        in_specs=[
            pl.BlockSpec(order.shape, lambda q, i: (0, 0)),
            pl.BlockSpec((lines.shape[0], step), lambda q, i: (0, q * steps + i)),
        ],
        out_specs=pl.BlockSpec((planes, many, slab, comps * BLOCK), lambda q, i: (0, i, q, 0)),
        compiler_params=pltpu.CompilerParams(vmem_limit_bytes=VMEM),
        cost_estimate=cost(SHORT),
        name="pack",
    )(order, lines)


def pack_apart_body(planes, comps, ways, given, extra, me_ref, order_ref, *rest):
    v_refs, o_refs = rest[:ways], rest[ways + given + extra :]
    rows = order_ref.shape[0]
    groups = v_refs[0].shape[0] // rows
    slab = groups * GROUP
    for g in range(groups):
        whole = jnp.concatenate([v_ref[g * rows : (g + 1) * rows, :] for v_ref in v_refs], axis=1)
        moved = mm(order_ref[...], whole).astype(BF16)
        spot = slice(g * GROUP, (g + 1) * GROUP)
        for k in range(ways):
            cells = slice(k * BLOCK, (k + 1) * BLOCK)
            if not given:
                place_rows(o_refs[k], moved, planes, comps, BLOCK, spot, cells)
                continue
            for y in range(planes):
                for c in range(comps):
                    at = (y * comps + c) * GROUP
                    to = c * slab + g * GROUP
                    o_refs[k][y, to : to + GROUP, :] = moved[at : at + GROUP, cells]
    if given:
        for k in range(ways):
            at = comps * slab
            for c in range(comps):
                o_refs[k][:, at + c * MOST : at + (c + 1) * MOST, :] = rest[ways][
                    k, :, :, c * BLOCK : (c + 1) * BLOCK
                ]
            o_refs[k][:, at + comps * MOST :, :] = rest[ways + 1][k]


def pack_apart(lines, order, me, chunk, planes, comps, ways, slab, after, marked=None):
    total = lines.shape[0]
    given = () if marked is None else marked
    shape = (planes, comps * slab + (comps + 1) * MOST, BLOCK) if given else (planes, slab, comps * BLOCK)
    return pl.pallas_call(
        functools.partial(pack_apart_body, planes, comps, ways, len(given), len(after)),
        out_shape=(jax.ShapeDtypeStruct(shape, BF16),) * ways,
        grid_spec=pltpu.PrefetchScalarGridSpec(
            num_scalar_prefetch=1,
            grid=(1,),
            in_specs=[pl.BlockSpec(order.shape, lambda i, m: (0, 0))]
            + [pl.BlockSpec((total, BLOCK), lambda i, m, k=k: (0, chunk * ways + (m[0] ^ k))) for k in range(ways)]
            + [pl.BlockSpec(x.shape, lambda i, m: (0, 0, 0, 0)) for x in given]
            + [pl.BlockSpec(memory_space=pltpu.HBM)] * len(after),
            out_specs=(pl.BlockSpec(shape, lambda i, m: (0, 0, 0)),) * ways,
        ),
        compiler_params=pltpu.CompilerParams(vmem_limit_bytes=VMEM),
        cost_estimate=cost(SHORT),
        name="pack_apart",
    )(me, order, *([lines] * ways), *given, *after)


def join_body(ways, *refs):
    for k in range(ways):
        refs[-1][:, k] = refs[k][...]


def join(pieces, after):
    ways = len(pieces)
    planes, height, cols = pieces[0].shape
    half = planes // 2
    return pl.pallas_call(
        functools.partial(join_body, ways),
        out_shape=jax.ShapeDtypeStruct((planes, ways, height, cols), BF16),
        grid=(2,),
        in_specs=[pl.BlockSpec((half, height, cols), lambda i: (i, 0, 0))] * ways
        + [pl.BlockSpec(memory_space=pltpu.HBM)] * len(after),
        out_specs=pl.BlockSpec((half, ways, height, cols), lambda i: (i, 0, 0, 0)),
        compiler_params=pltpu.CompilerParams(vmem_limit_bytes=VMEM),
        cost_estimate=cost(LONG),
        name="join",
    )(*pieces, *after)


def split_body(ways, count, x_ref, *rest):
    for k in range(1, ways):
        rest[count + k - 1][...] = x_ref[:, k]


def split(x, quarter, slab, after):
    planes, ways, _, cols = x.shape
    half = planes // 2
    return pl.pallas_call(
        functools.partial(split_body, ways, len(after)),
        out_shape=(jax.ShapeDtypeStruct((planes, slab, cols), BF16),) * (ways - 1),
        grid=(2,),
        in_specs=[pl.BlockSpec((half, ways, slab, cols), lambda i: (i, 0, quarter, 0))]
        + [pl.BlockSpec(memory_space=pltpu.HBM)] * len(after),
        out_specs=(pl.BlockSpec((half, slab, cols), lambda i: (i, 0, 0)),) * (ways - 1),
        compiler_params=pltpu.CompilerParams(vmem_limit_bytes=VMEM),
        cost_estimate=cost(SHORT),
        name="split",
    )(x, *after)


def depth_body(count, slab, block, extra, near_in, near_out, me_ref, x_ref, d_ref, m_ref, *rest):
    o_ref, s_ref, g_ref = rest[extra:]
    tall, ways, height, cols = x_ref.shape
    stacked = cols == BLOCK
    cols = 3 * BLOCK
    wide = cols // 3
    phase = pl.program_id(0)
    step = pl.program_id(1)
    spot = pl.ds(pl.multiple_of(step * block, block), block)
    me = me_ref[0]

    @pl.when((phase == 0) & (step == 0))
    def _():
        for r in range(tall):
            for k in range(ways):
                to = pl.multiple_of((r * ways + (me ^ k if near_in else k)) * slab, slab)
                for q in range(1 if stacked else count):
                    s_ref[pl.ds(to, slab), q * cols : (q + 1) * cols] = (
                        jnp.concatenate([x_ref[r, k, c * slab : (c + 1) * slab] for c in range(3)], axis=1)
                        if stacked
                        else x_ref[r, k, q * slab : (q + 1) * slab]
                    )

    @pl.when(phase == 0)
    def _():
        g_ref[spot, :] = (mm(d_ref[...], s_ref[...]) * m_ref[spot, :]).astype(BF16)

    @pl.when(phase == 1)
    def _():
        curv = mm(d_ref[...], g_ref[...]) * m_ref[spot, :]
        grad = g_ref[spot, :].astype(F32)
        each = block // slab
        for q in range(count):
            upward = s_ref[spot, q * cols + 2 * wide : q * cols + 3 * wide].astype(F32)
            for c in range(3):
                part = slice(q * cols + c * wide, q * cols + (c + 1) * wide)
                term = (viscosity * curv[:, part] - upward * grad[:, part]).astype(BF16)
                for n in range(each):
                    r = step * (each // ways) + n // ways
                    k = me ^ (n % ways) if near_out else n % ways
                    o_ref[r, k, q * slab : (q + 1) * slab, c * wide : (c + 1) * wide] = term[
                        n * slab : (n + 1) * slab, :
                    ]


def depth(x, me, deriv_z, metric_z, count, slab, near_in, near_out, after, place=0, total=None, held=()):
    tall, ways, _, cols = x.shape
    given = (tall, ways, count * slab if cols > BLOCK else 3 * slab, cols)
    cols = 3 * BLOCK
    shape = (tall, ways, count * slab, cols)
    extra = tuple(held) + tuple(after)
    height = deriv_z.shape[0]
    block = 512
    return pl.pallas_call(
        functools.partial(depth_body, count, slab, block, len(extra), near_in, near_out),
        out_shape=jax.ShapeDtypeStruct((tall, ways, (total or count) * slab, cols), BF16),
        grid_spec=pltpu.PrefetchScalarGridSpec(
            num_scalar_prefetch=1,
            grid=(2, height // block),
            in_specs=[
                pl.BlockSpec(given, lambda p, i, m: (0, 0, 0, 0)),
                pl.BlockSpec((block, height), lambda p, i, m: (i, 0)),
                pl.BlockSpec((height, 1), lambda p, i, m: (0, 0)),
            ]
            + [pl.BlockSpec(memory_space=pltpu.HBM)] * len(extra),
            out_specs=pl.BlockSpec(shape, lambda p, i, m: (0, 0, place, 0)),
            scratch_shapes=[pltpu.VMEM((height, count * cols), BF16), pltpu.VMEM((height, count * cols), BF16)],
        ),
        input_output_aliases={4: 0} if held else {},
        compiler_params=pltpu.CompilerParams(vmem_limit_bytes=VMEM),
        cost_estimate=cost(SHORT),
        name="depth",
    )(me, x, deriv_z, metric_z, *extra)


def marker_body(capacity, ways, apart, count_ref, me_ref, owner_row, owner_col, block_col, t_ref, o_ref, *l_refs):
    earlier = lax.broadcasted_iota(jnp.int32, (capacity, capacity), 0)
    later = lax.broadcasted_iota(jnp.int32, (capacity, capacity), 1)
    same = (owner_col[...] == owner_row[...]) & (earlier < later)
    position = jnp.sum(same.astype(jnp.int32), axis=0, keepdims=True)
    slot = lax.broadcasted_iota(jnp.int32, (1, capacity), 1)
    owner = owner_row[...]
    places = o_ref.shape[0]
    if apart:
        owner = ((owner % ways) ^ me_ref[0]) * (places // (ways * MOST)) + owner // ways
    slotted = jnp.where(slot < count_ref[0], owner * MOST + position, places)
    placing = (lax.broadcasted_iota(jnp.int32, (places, capacity), 0) == slotted).astype(F32).astype(BF16)
    for c in range(3):
        o_ref[:, c * BLOCK : (c + 1) * BLOCK] = mm(placing, t_ref[c]).astype(BF16)
    lane = lax.broadcasted_iota(jnp.int32, (capacity, BLOCK), 1)
    high = block_col[...] // 128
    low = block_col[...] - high * 128
    label = jnp.where(lane == 0, high, jnp.where(lane == 1, low, jnp.where(lane == 2, 1, 0)))
    label = mm(placing, label.astype(F32).astype(BF16)).astype(BF16)
    if apart:
        l_refs[0][...] = label
    else:
        o_ref[:, 3 * BLOCK :] = label


def markers(ib_target, ib_owner, ib_block, ib_count, me, devices, ways, apart):
    capacity = ib_owner.shape[1]
    places = devices * MOST
    if apart:
        shapes = (jax.ShapeDtypeStruct((places, 3 * BLOCK), BF16),)
        shapes += (jax.ShapeDtypeStruct((places, BLOCK), BF16),)
    else:
        shapes = (jax.ShapeDtypeStruct((places, 4 * BLOCK), BF16),)
    return pl.pallas_call(
        functools.partial(marker_body, capacity, ways, apart),
        out_shape=shapes,
        in_specs=[pl.BlockSpec(memory_space=pltpu.SMEM)] * 2 + [pl.BlockSpec(memory_space=pltpu.VMEM)] * 4,
        out_specs=(pl.BlockSpec(memory_space=pltpu.VMEM),) * len(shapes),
        compiler_params=pltpu.CompilerParams(vmem_limit_bytes=VMEM),
        cost_estimate=cost(SHORT),
        name="markers",
    )(
        ib_count,
        me,
        ib_owner,
        ib_owner.reshape(capacity, 1),
        ib_block.reshape(capacity, 1),
        jnp.transpose(ib_target[0], (1, 0, 2)),
    )


def near_body(planes, comps, extra, near_columns, v_ref, dx_ref, dy_ref, mx_ref, my_ref, *rest):
    p_refs, (g_ref, band_ref, scale_ref) = rest[extra:-3], rest[-3:]
    rows, columns = v_ref.shape
    group = rows // (planes * comps)
    part = 512

    @pl.when(pl.program_id(0) == 0)
    def _():
        row = lax.broadcasted_iota(jnp.int32, (rows, planes), 0) % planes
        take = (row == lax.broadcasted_iota(jnp.int32, (rows, planes), 1)).astype(F32)
        scale_ref[...] = jnp.sum(take * my_ref[...], axis=1, keepdims=True)
        take = take.astype(BF16)
        spread = mm_nt(mm(take, dy_ref[...]).astype(BF16), take)
        one = lax.broadcasted_iota(jnp.int32, (rows, rows), 0) // planes
        other = lax.broadcasted_iota(jnp.int32, (rows, rows), 1) // planes
        band_ref[...] = jnp.where(one == other, spread, 0.0).astype(BF16)

    for j in range(columns // part):
        span = slice(j * part, (j + 1) * part)
        g_ref[:, span] = (mm_nt(v_ref[...], dx_ref[span, :]) * mx_ref[:, span]).astype(BF16)
    for j in range(columns // part):
        span = slice(j * part, (j + 1) * part)
        curv = mm_nt(g_ref[...], dx_ref[span, :]) * mx_ref[:, span]
        vel = v_ref[:, span]
        grad_y = (mm(band_ref[...], vel) * scale_ref[...]).astype(BF16)
        curv = curv + mm(band_ref[...], grad_y) * scale_ref[...]
        shape = (group, comps, planes, part)
        vel = vel.astype(F32).reshape(shape)
        grad_y = grad_y.astype(F32).reshape(shape)
        grad_x = g_ref[:, span].astype(F32).reshape(shape)
        curv = curv.reshape(shape)
        tendency = viscosity * curv - (vel[:, 0:1] * grad_x + vel[:, 1:2] * grad_y)
        at = j * part
        if at < near_columns:
            p_refs[0][:, :, :, span] = vel + time_step * tendency
        else:
            p_refs[-1][:, :, :, at - near_columns : at - near_columns + part] = vel + time_step * tendency


def near(lines, deriv_x, deriv_y, metric_x, metric_y, planes, comps, slab, near_columns, after):
    total, columns = lines.shape
    rows = GROUP * planes * comps
    far = columns - near_columns
    shapes = ((columns, near_columns), (far, far)) if near_columns else ((far, far),)
    return pl.pallas_call(
        functools.partial(near_body, planes, comps, len(after), near_columns),
        out_shape=tuple(jax.ShapeDtypeStruct((slab, comps, planes, n), F32) for n, _ in shapes),
        grid=(total // rows,),
        in_specs=[
            pl.BlockSpec((rows, columns), lambda i: (i, 0)),
            pl.BlockSpec(deriv_x.shape, lambda i: (0, 0), pipeline_mode=pl.Buffered(1)),
            pl.BlockSpec(deriv_y.shape, lambda i: (0, 0)),
            pl.BlockSpec((1, columns), lambda i: (0, 0)),
            pl.BlockSpec((1, planes), lambda i: (0, 0)),
        ]
        + [pl.BlockSpec(memory_space=pltpu.HBM)] * len(after),
        out_specs=tuple(pl.BlockSpec((GROUP, comps, planes, n), lambda i: (i, 0, 0, 0)) for _, n in shapes),
        scratch_shapes=[
            pltpu.VMEM((rows, columns), BF16),
            pltpu.VMEM((rows, rows), BF16),
            pltpu.VMEM((rows, 1), F32),
        ],
        compiler_params=pltpu.CompilerParams(vmem_limit_bytes=VMEM),
        cost_estimate=cost(SHORT),
        name="near",
    )(lines, deriv_x, deriv_y, metric_x, metric_y, *after)


def ready_markers(got_ref, s_ref, l_ref):
    lane = lax.broadcasted_iota(jnp.int32, (8, BLOCK), 1)
    pick = jnp.where(lane == 0, 128.0, jnp.where(lane < 3, 1.0, 0.0)).astype(BF16)
    slots = s_ref.shape[0]
    if len(got_ref.shape) == 4:
        values = [got_ref[:, :, c * MOST : (c + 1) * MOST, :] for c in range(4)]
    else:
        values = [got_ref[:, :, c * BLOCK : (c + 1) * BLOCK] for c in range(4)]
    values = [x.astype(F32).reshape(slots, BLOCK).astype(BF16) for x in values]
    l_ref[...] = mm_nt(pick, values[3]).astype(jnp.int32)
    for c in range(3):
        s_ref[:, c * BLOCK : (c + 1) * BLOCK] = values[c]
    s_ref[:, 3 * BLOCK :] = jnp.ones((slots, BLOCK), BF16)


def markers_spec(got, slab):
    if got.ndim == 4:
        rows = 4 * MOST
        block = (got.shape[0], got.shape[1], rows, got.shape[3])
        return pl.BlockSpec(block, lambda *_: (0, 0, 3 * slab // rows, 0)), got.shape[0] * got.shape[1] * MOST
    return pl.BlockSpec(got.shape, lambda *_: (0, 0, 0)), got.shape[0] * MOST


def settle(order_ref, taken, s_ref, l_ref, p_ref, o_ref, comps, wide, group, xblocks, first, at):
    slab = p_ref.shape[0]
    planes = p_ref.shape[2]
    lines = group * planes
    slots = s_ref.shape[0]
    label = l_ref[0:1, :]
    for g in range(slab // group):
        some = slice(g * group, (g + 1) * group)
        moved = mm(order_ref[...], taken(some).reshape(lines, comps * wide)) * time_step
        line = (g * lines + lax.broadcasted_iota(jnp.int32, (lines, slots), 0)) * xblocks + 1
        for b in range(wide // BLOCK):
            chosen = (line + (first + b) == label).astype(F32).astype(BF16)
            share = mm(chosen, s_ref[...])
            inverse = 1.0 / (1.0 + share[:, 3 * BLOCK :])
            cells = slice(at + b * BLOCK, at + (b + 1) * BLOCK)
            for c in range(comps):
                term = moved[:, c * wide + b * BLOCK : c * wide + (b + 1) * BLOCK]
                total = p_ref[some, c, :, cells].reshape(lines, BLOCK) + term + share[:, c * BLOCK : (c + 1) * BLOCK]
                o_ref[some, c, :, cells] = (total * inverse).reshape(group, planes, BLOCK)


def mark_body(planes, comps, group, xblocks, start, got_ref, p_ref, o_ref, i_ref, s_ref, l_ref):
    step = pl.program_id(0)

    @pl.when(step == 0)
    def _():
        ready_markers(got_ref, s_ref, l_ref)

    blocks = p_ref.shape[3] // BLOCK
    lines = group * planes
    slots = s_ref.shape[0]
    for b in range(blocks):
        cells = slice(b * BLOCK, (b + 1) * BLOCK)
        for g in range(p_ref.shape[0] // group):
            some = slice(g * group, (g + 1) * group)
            line = (g * lines + lax.broadcasted_iota(jnp.int32, (lines, slots), 0)) * xblocks + 1
            chosen = (line + (start + step * blocks + b) == l_ref[0:1, :]).astype(F32).astype(BF16)
            share = mm(chosen, s_ref[...])
            inverse = 1.0 / (1.0 + share[:, 3 * BLOCK :])
            i_ref[some, :, cells] = (time_step * inverse).reshape(group, planes, BLOCK)
            for c in range(comps):
                total = p_ref[some, c, :, cells].reshape(lines, BLOCK) + share[:, c * BLOCK : (c + 1) * BLOCK]
                o_ref[some, c, :, cells] = (total * inverse).reshape(group, planes, BLOCK)


def mark(far, got, columns, group, after):
    slab, comps, planes, wide = far.shape
    step = 2 * BLOCK
    spec = pl.BlockSpec((slab, comps, planes, step), lambda i: (0, 0, 0, i))
    got_spec, slots = markers_spec(got, slab)

    def body(*refs):
        start = (columns - wide) // BLOCK
        mark_body(planes, comps, group, columns // BLOCK, start, *refs[:2], *refs[2 + len(after) :])

    return pl.pallas_call(
        body,
        out_shape=(
            jax.ShapeDtypeStruct(far.shape, F32),
            jax.ShapeDtypeStruct((slab, planes, wide), F32),
        ),
        grid=(wide // step,),
        in_specs=[got_spec, spec] + [pl.BlockSpec(memory_space=pltpu.HBM)] * len(after),
        out_specs=(spec, pl.BlockSpec((slab, planes, step), lambda i: (0, 0, i))),
        scratch_shapes=[pltpu.VMEM((slots, 4 * BLOCK), BF16), pltpu.VMEM((8, slots), jnp.int32)],
        compiler_params=pltpu.CompilerParams(vmem_limit_bytes=ROOM),
        cost_estimate=cost(SHORT),
        name="mark",
    )(got, far, *after)


def last_body(planes, comps, count, extra, order_ref, *rest):
    r_refs, (i_ref, p_ref), o_ref = rest[:count], rest[count : count + 2], rest[count + 2 + extra]
    group = p_ref.shape[0]
    groups = r_refs[0].shape[1]
    lines = group * planes
    for q in range(count):
        for xg in range(groups):
            at = (q * groups + xg) * BLOCK
            cells = slice(at, at + BLOCK)
            moved = mm(order_ref[...], r_refs[q][:, xg].reshape(lines, comps * BLOCK))
            weight = i_ref[:, :, cells]
            for c in range(comps):
                term = moved[:, c * BLOCK : (c + 1) * BLOCK].reshape(group, planes, BLOCK)
                o_ref[:, c, :, cells] = p_ref[:, c, :, cells] + term * weight


def last(field, far, weight, returned, order):
    slab, comps, planes, wide = far.shape
    groups = returned.shape[1]
    count = wide // (groups * BLOCK)
    steps = slab // GROUP
    columns = wide if field is None else field.shape[3]
    skip = columns // wide - 1
    held = () if field is None else (field,)
    return pl.pallas_call(
        functools.partial(last_body, planes, comps, count, len(held)),
        out_shape=jax.ShapeDtypeStruct((slab, comps, planes, columns), F32),
        grid=(steps,),
        in_specs=[pl.BlockSpec(order.shape, lambda i: (0, 0))]
        + [
            pl.BlockSpec((planes, groups, GROUP, comps * BLOCK), lambda i, q=q: (0, 0, q * steps + i, 0))
            for q in range(count)
        ]
        + [
            pl.BlockSpec((GROUP, planes, wide), lambda i: (i, 0, 0)),
            pl.BlockSpec((GROUP, comps, planes, wide), lambda i: (i, 0, 0, 0)),
        ]
        + [pl.BlockSpec(memory_space=pltpu.HBM)] * len(held),
        out_specs=pl.BlockSpec((GROUP, comps, planes, wide), lambda i: (i, 0, 0, skip)),
        input_output_aliases={3 + count: 0} if held else {},
        compiler_params=pltpu.CompilerParams(vmem_limit_bytes=ROOM),
        cost_estimate=cost(SHORT),
        name="last",
    )(order, *([returned] * count), weight, far, *held)


def last_apart_body(comps, group, xblocks, start, ways, me_ref, order_ref, got_ref, own_ref, *rest):
    pieces, p_ref = rest[: ways - 1], rest[ways - 1]
    o_ref, s_ref, l_ref, t_ref = rest[-4:]
    step = pl.program_id(0)

    @pl.when(step == 0)
    def _():
        ready_markers(got_ref, s_ref, l_ref)
        t_ref[...] = own_ref[:, 0]

    for k in range(1, ways):

        @pl.when(step == k)
        def _(k=k):
            t_ref[...] = pieces[k - 1][...]

    settle(
        order_ref,
        lambda some: t_ref[:, some, :],
        s_ref,
        l_ref,
        p_ref,
        o_ref,
        comps,
        BLOCK,
        group,
        xblocks,
        start + (me_ref[0] ^ step),
        0,
    )


def last_apart(field, own, pieces, got, order, me, chunk, group, after):
    slab, comps, planes, columns = field.shape
    ways = own.shape[1]
    spec = pl.BlockSpec((slab, comps, planes, BLOCK), lambda i, m: (0, 0, 0, chunk * ways + (m[0] ^ i)))
    whole = pl.BlockSpec((planes, slab, comps * BLOCK), lambda i, m: (0, 0, 0))
    got_spec, slots = markers_spec(got, slab)
    return pl.pallas_call(
        functools.partial(last_apart_body, comps, group, columns // BLOCK, chunk * ways, ways),
        out_shape=jax.ShapeDtypeStruct(field.shape, F32),
        grid_spec=pltpu.PrefetchScalarGridSpec(
            num_scalar_prefetch=1,
            grid=(ways,),
            in_specs=[
                pl.BlockSpec(order.shape, lambda i, m: (0, 0)),
                got_spec,
                pl.BlockSpec((planes, 1, slab, comps * BLOCK), lambda i, m: (0, 0, chunk, 0)),
            ]
            + [whole] * (ways - 1)
            + [spec]
            + [pl.BlockSpec(memory_space=pltpu.HBM)] * len(after),
            out_specs=spec,
            scratch_shapes=[
                pltpu.VMEM((slots, 4 * BLOCK), BF16),
                pltpu.VMEM((8, slots), jnp.int32),
                pltpu.VMEM((planes, slab, comps * BLOCK), BF16),
            ],
        ),
        input_output_aliases={4 + ways - 1: 0},
        compiler_params=pltpu.CompilerParams(vmem_limit_bytes=VMEM),
        cost_estimate=cost(LONG),
        name="last_apart",
    )(me, order, got, own, *pieces, field, *after)


def come_body(count, *refs):
    refs[count][...] = jnp.zeros_like(refs[count])


def come(pieces):
    return pl.pallas_call(
        functools.partial(come_body, len(pieces)),
        out_shape=jax.ShapeDtypeStruct((8, BLOCK), F32),
        in_specs=[pl.BlockSpec(memory_space=pltpu.HBM)] * len(pieces),
        out_specs=pl.BlockSpec(memory_space=pltpu.VMEM),
        cost_estimate=cost(LONG),
        name="come",
    )(*pieces)


def across(pieces):
    ways = lax.axis_size("col")
    return tuple(
        lax.ppermute(piece, "col", [(c, c ^ k) for c in range(ways)]) for k, piece in enumerate(pieces, 1)
    )


def along(x):
    return lax.all_to_all(x, "row", split_axis=0, concat_axis=0, tiled=True)


def exchange(x):
    return lax.all_to_all(x, AXES, split_axis=0, concat_axis=0, tiled=True)


def local(
    velocity,
    deriv_x,
    deriv_y,
    deriv_z,
    metric_x,
    metric_y,
    metric_z,
    ib_target,
    ib_owner,
    ib_block,
    ib_count,
):
    slab, planes, comps, columns = velocity.shape
    row_count, ways = lax.axis_size("row"), lax.axis_size("col")
    devices = row_count * ways
    groups = devices // planes
    group = min(32, slab)
    chunks = columns // (groups * BLOCK)
    me = lax.axis_index("col").astype(jnp.int32).reshape(1)
    lines = jnp.transpose(velocity, (0, 2, 1, 3)).reshape(slab * comps * planes, columns)
    order = jnp.asarray(pack_order(planes, comps), BF16)
    back = jnp.asarray(unpack_order(planes, group), BF16)
    small = jnp.asarray(unpack_order(planes, GROUP), BF16)
    metric_col = metric_z[:, None]
    apart = row_count == planes and chunks == QUARTERS and slab == QUARTERS * GROUP
    marked, *labels = markers(ib_target, ib_owner, ib_block, ib_count, me, devices, ways, apart)
    at_once = 2 if apart else chunks
    near_columns = columns // 2 if apart else 0
    first = pack(lines, order, at_once, planes, comps, groups, slab)
    block = (devices,) + first.shape[2:]
    arrived = exchange(first.reshape(block)).reshape((row_count, ways) + first.shape[2:])
    *fields, far = near(
        lines, deriv_x, deriv_y, metric_x[None, :], metric_y[None, :], planes, comps, slab, near_columns, (first,)
    )

    if not apart:
        got = exchange(marked.reshape(devices, MOST, 4 * BLOCK))
        terms = depth(arrived, me, deriv_z, metric_col, at_once, slab, False, False, (far,))
        home = exchange(terms.reshape(block)).reshape(first.shape)
        far, weight = mark(far, got, columns, group, ())
        return jnp.transpose(last(None, far, weight, home, small), (0, 2, 1, 3))

    def outward(k, after, marked=None):
        return pack_apart(lines, order, me, k, planes, comps, ways, slab, after, marked)

    (field,) = fields
    marked = (marked.reshape(ways, planes, MOST, comps * BLOCK), labels[0].reshape(ways, planes, MOST, BLOCK))
    sent3 = outward(3, (field,))
    sent2 = outward(2, (sent3[0],), marked)
    later2, later3 = lax.optimization_barrier((sent2[EARLY:], sent3[EARLY:], arrived))[:2]
    come2 = across(tuple(sent2[1:EARLY]) + tuple(later2))
    come3 = across(tuple(sent3[1:EARLY]) + tuple(later3))
    terms = depth(arrived, me, deriv_z, metric_col, 2, slab, False, True, (sent2[0],))
    home = along(terms)
    joined2 = join((sent2[0],) + come2, (terms,))
    split0 = split(home, 0, slab, (joined2,))
    back0 = across(split0)
    split1 = split(home, 1, slab, (split0[0],))
    back1 = across(split1)
    got = full2 = along(joined2)
    joined3 = join((sent3[0],) + come3, (split1[0],))
    full3 = along(joined3)
    terms = depth(full2, me, deriv_z, metric_col, 1, slab, True, False, (joined3,), 0, 2)
    terms = depth(full3, me, deriv_z, metric_col, 1, slab, True, False, (come(back0),), 1, 2, (terms,))
    home_all = exchange(terms.reshape(block)).reshape(first.shape)
    field = last_apart(field, home, back0, got, back, me, 0, group, (terms,))
    field = last_apart(field, home, back1, got, back, me, 1, group, ())
    far, weight = mark(far, got, columns, group, (field,))
    return jnp.transpose(last(field, far, weight, home_all, small), (0, 2, 1, 3))


def solution(mesh):
    in_specs = (
        P(AXES, None, None, None),
        P(),
        P(),
        P(),
        P(),
        P(),
        P(),
        P(AXES, None, None, None),
        P(AXES, None),
        P(AXES, None),
        P(AXES),
    )
    out_specs = P(AXES, None, None, None)
    return jax.shard_map(local, mesh=mesh, in_specs=in_specs, out_specs=out_specs, check_vma=False)
```

```python
import functools

import jax
import jax.numpy as jnp
import numpy as np
from jax import lax
from jax.experimental import pallas as pl
from jax.experimental.pallas import tpu as pltpu
from jax.sharding import PartitionSpec as P

BLOCK = 128
MOST = 8
GROUP = 16
QUARTERS = 4
VMEM = 60 << 20
ROOM = 60 << 20
LAST = 16
SHORT = 1
EARLY = 2
PACK = 4
LONG = 10**12

viscosity = 0.4
time_step = 0.2

F32 = jnp.float32
BF16 = jnp.bfloat16
AXES = ("row", "col")


def cost(flops):
    return pl.CostEstimate(flops=flops, bytes_accessed=1, transcendentals=0)


def mm(a, b):
    return lax.dot_general(a, b, (((1,), (0,)), ((), ())), preferred_element_type=F32)


def mm_nt(a, b):
    return lax.dot_general(a, b, (((1,), (1,)), ((), ())), preferred_element_type=F32)


def pack_order(planes, comps, group):
    rows = group * planes * comps
    table = np.zeros((rows, rows), np.float32)
    for y in range(planes):
        for c in range(comps):
            for z in range(group):
                table[(y * comps + c) * group + z, (z * comps + c) * planes + y] = 1
    return table


def unpack_order(planes, group):
    rows = group * planes
    table = np.zeros((rows, rows), np.float32)
    for y in range(planes):
        for z in range(group):
            table[z * planes + y, y * group + z] = 1
    return table


def place_rows(o_ref, moved, planes, comps, wide, at_rows, spot):
    for y in range(planes):
        for c in range(comps):
            group = moved.shape[0] // (planes * comps)
            at = (y * comps + c) * group
            o_ref[y, at_rows, c * wide : (c + 1) * wide] = moved[at : at + group, spot]


def pack_body(planes, comps, wide, order_ref, v_ref, o_ref):
    lanes = v_ref.shape[1]
    rows = order_ref.shape[0]
    group = rows // (planes * comps)
    for g in range(v_ref.shape[0] // rows):
        moved = mm(order_ref[...], v_ref[g * rows : (g + 1) * rows, :]).astype(BF16)
        for xg in range(lanes // wide):
            place_rows(
                o_ref.at[:, xg],
                moved,
                planes,
                comps,
                wide,
                slice(g * group, (g + 1) * group),
                slice(xg * wide, (xg + 1) * wide),
            )


def pack(lines, order, count, planes, comps, groups, slab):
    many = PACK
    step = many * BLOCK
    steps = groups // many
    return pl.pallas_call(
        functools.partial(pack_body, planes, comps, BLOCK),
        out_shape=jax.ShapeDtypeStruct((planes, groups, count * slab, comps * BLOCK), BF16),
        grid=(count, steps),
        in_specs=[
            pl.BlockSpec(order.shape, lambda q, i: (0, 0)),
            pl.BlockSpec((lines.shape[0], step), lambda q, i: (0, q * steps + i)),
        ],
        out_specs=pl.BlockSpec((planes, many, slab, comps * BLOCK), lambda q, i: (0, i, q, 0)),
        compiler_params=pltpu.CompilerParams(vmem_limit_bytes=VMEM),
        cost_estimate=cost(SHORT),
        name="pack",
    )(order, lines)


def pack_apart_body(planes, comps, ways, given, extra, me_ref, order_ref, *rest):
    v_refs, o_refs = rest[:ways], rest[ways + given + extra :]
    rows = order_ref.shape[0]
    groups = v_refs[0].shape[0] // rows
    slab = groups * GROUP
    for g in range(groups):
        whole = jnp.concatenate([v_ref[g * rows : (g + 1) * rows, :] for v_ref in v_refs], axis=1)
        moved = mm(order_ref[...], whole).astype(BF16)
        spot = slice(g * GROUP, (g + 1) * GROUP)
        for k in range(ways):
            cells = slice(k * BLOCK, (k + 1) * BLOCK)
            if not given:
                place_rows(o_refs[k], moved, planes, comps, BLOCK, spot, cells)
                continue
            for y in range(planes):
                for c in range(comps):
                    at = (y * comps + c) * GROUP
                    to = c * slab + g * GROUP
                    o_refs[k][y, to : to + GROUP, :] = moved[at : at + GROUP, cells]
    if given:
        for k in range(ways):
            at = comps * slab
            for c in range(comps):
                o_refs[k][:, at + c * MOST : at + (c + 1) * MOST, :] = rest[ways][
                    k, :, :, c * BLOCK : (c + 1) * BLOCK
                ]
            o_refs[k][:, at + comps * MOST :, :] = rest[ways + 1][k]


def pack_apart(lines, order, me, chunk, planes, comps, ways, slab, after, marked=None):
    total = lines.shape[0]
    given = () if marked is None else marked
    shape = (planes, comps * slab + (comps + 1) * MOST, BLOCK) if given else (planes, slab, comps * BLOCK)
    return pl.pallas_call(
        functools.partial(pack_apart_body, planes, comps, ways, len(given), len(after)),
        out_shape=(jax.ShapeDtypeStruct(shape, BF16),) * ways,
        grid_spec=pltpu.PrefetchScalarGridSpec(
            num_scalar_prefetch=1,
            grid=(1,),
            in_specs=[pl.BlockSpec(order.shape, lambda i, m: (0, 0))]
            + [pl.BlockSpec((total, BLOCK), lambda i, m, k=k: (0, chunk * ways + (m[0] ^ k))) for k in range(ways)]
            + [pl.BlockSpec(x.shape, lambda i, m: (0, 0, 0, 0)) for x in given]
            + [pl.BlockSpec(memory_space=pltpu.HBM)] * len(after),
            out_specs=(pl.BlockSpec(shape, lambda i, m: (0, 0, 0)),) * ways,
        ),
        compiler_params=pltpu.CompilerParams(vmem_limit_bytes=VMEM),
        cost_estimate=cost(SHORT),
        name="pack_apart",
    )(me, order, *([lines] * ways), *given, *after)


def join_body(ways, *refs):
    for k in range(ways):
        refs[-1][:, k] = refs[k][...]


def join(pieces, after):
    ways = len(pieces)
    planes, height, cols = pieces[0].shape
    half = planes // 2
    return pl.pallas_call(
        functools.partial(join_body, ways),
        out_shape=jax.ShapeDtypeStruct((planes, ways, height, cols), BF16),
        grid=(2,),
        in_specs=[pl.BlockSpec((half, height, cols), lambda i: (i, 0, 0))] * ways
        + [pl.BlockSpec(memory_space=pltpu.HBM)] * len(after),
        out_specs=pl.BlockSpec((half, ways, height, cols), lambda i: (i, 0, 0, 0)),
        compiler_params=pltpu.CompilerParams(vmem_limit_bytes=VMEM),
        cost_estimate=cost(LONG),
        name="join",
    )(*pieces, *after)


def split_body(ways, count, x_ref, *rest):
    for k in range(1, ways):
        rest[count + k - 1][...] = x_ref[:, k]


def split(x, quarter, slab, after):
    planes, ways, _, cols = x.shape
    half = planes // 2
    return pl.pallas_call(
        functools.partial(split_body, ways, len(after)),
        out_shape=(jax.ShapeDtypeStruct((planes, slab, cols), BF16),) * (ways - 1),
        grid=(2,),
        in_specs=[pl.BlockSpec((half, ways, slab, cols), lambda i: (i, 0, quarter, 0))]
        + [pl.BlockSpec(memory_space=pltpu.HBM)] * len(after),
        out_specs=(pl.BlockSpec((half, slab, cols), lambda i: (i, 0, 0)),) * (ways - 1),
        compiler_params=pltpu.CompilerParams(vmem_limit_bytes=VMEM),
        cost_estimate=cost(SHORT),
        name="split",
    )(x, *after)


def depth_body(count, slab, block, extra, near_in, near_out, me_ref, x_ref, d_ref, m_ref, *rest):
    o_ref, s_ref, g_ref = rest[extra:]
    tall, ways, height, cols = x_ref.shape
    stacked = cols == BLOCK
    cols = 3 * BLOCK
    wide = cols // 3
    phase = pl.program_id(0)
    step = pl.program_id(1)
    spot = pl.ds(pl.multiple_of(step * block, block), block)
    me = me_ref[0]

    @pl.when((phase == 0) & (step == 0))
    def _():
        for r in range(tall):
            for k in range(ways):
                to = pl.multiple_of((r * ways + (me ^ k if near_in else k)) * slab, slab)
                for q in range(1 if stacked else count):
                    s_ref[pl.ds(to, slab), q * cols : (q + 1) * cols] = (
                        jnp.concatenate([x_ref[r, k, c * slab : (c + 1) * slab] for c in range(3)], axis=1)
                        if stacked
                        else x_ref[r, k, q * slab : (q + 1) * slab]
                    )

    @pl.when(phase == 0)
    def _():
        g_ref[spot, :] = (mm(d_ref[...], s_ref[...]) * m_ref[spot, :]).astype(BF16)

    @pl.when(phase == 1)
    def _():
        curv = mm(d_ref[...], g_ref[...]) * m_ref[spot, :]
        grad = g_ref[spot, :].astype(F32)
        each = block // slab
        for q in range(count):
            upward = s_ref[spot, q * cols + 2 * wide : q * cols + 3 * wide].astype(F32)
            for c in range(3):
                part = slice(q * cols + c * wide, q * cols + (c + 1) * wide)
                term = (viscosity * curv[:, part] - upward * grad[:, part]).astype(BF16)
                for n in range(each):
                    r = step * (each // ways) + n // ways
                    k = me ^ (n % ways) if near_out else n % ways
                    o_ref[r, k, q * slab : (q + 1) * slab, c * wide : (c + 1) * wide] = term[
                        n * slab : (n + 1) * slab, :
                    ]


def depth(x, me, deriv_z, metric_z, count, slab, near_in, near_out, after, place=0, total=None, held=()):
    tall, ways, _, cols = x.shape
    given = (tall, ways, count * slab if cols > BLOCK else 3 * slab, cols)
    cols = 3 * BLOCK
    shape = (tall, ways, count * slab, cols)
    extra = tuple(held) + tuple(after)
    height = deriv_z.shape[0]
    block = 512
    return pl.pallas_call(
        functools.partial(depth_body, count, slab, block, len(extra), near_in, near_out),
        out_shape=jax.ShapeDtypeStruct((tall, ways, (total or count) * slab, cols), BF16),
        grid_spec=pltpu.PrefetchScalarGridSpec(
            num_scalar_prefetch=1,
            grid=(2, height // block),
            in_specs=[
                pl.BlockSpec(given, lambda p, i, m: (0, 0, 0, 0)),
                pl.BlockSpec((block, height), lambda p, i, m: (i, 0)),
                pl.BlockSpec((height, 1), lambda p, i, m: (0, 0)),
            ]
            + [pl.BlockSpec(memory_space=pltpu.HBM)] * len(extra),
            out_specs=pl.BlockSpec(shape, lambda p, i, m: (0, 0, place, 0)),
            scratch_shapes=[pltpu.VMEM((height, count * cols), BF16), pltpu.VMEM((height, count * cols), BF16)],
        ),
        input_output_aliases={4: 0} if held else {},
        compiler_params=pltpu.CompilerParams(vmem_limit_bytes=VMEM),
        cost_estimate=cost(SHORT),
        name="depth",
    )(me, x, deriv_z, metric_z, *extra)


def marker_body(capacity, ways, apart, count_ref, me_ref, owner_row, owner_col, block_col, t_ref, o_ref, *l_refs):
    earlier = lax.broadcasted_iota(jnp.int32, (capacity, capacity), 0)
    later = lax.broadcasted_iota(jnp.int32, (capacity, capacity), 1)
    same = (owner_col[...] == owner_row[...]) & (earlier < later)
    position = jnp.sum(same.astype(jnp.int32), axis=0, keepdims=True)
    slot = lax.broadcasted_iota(jnp.int32, (1, capacity), 1)
    owner = owner_row[...]
    places = o_ref.shape[0]
    if apart:
        owner = ((owner % ways) ^ me_ref[0]) * (places // (ways * MOST)) + owner // ways
    slotted = jnp.where(slot < count_ref[0], owner * MOST + position, places)
    placing = (lax.broadcasted_iota(jnp.int32, (places, capacity), 0) == slotted).astype(F32).astype(BF16)
    for c in range(3):
        o_ref[:, c * BLOCK : (c + 1) * BLOCK] = mm(placing, t_ref[c]).astype(BF16)
    lane = lax.broadcasted_iota(jnp.int32, (capacity, BLOCK), 1)
    high = block_col[...] // 128
    low = block_col[...] - high * 128
    label = jnp.where(lane == 0, high, jnp.where(lane == 1, low, jnp.where(lane == 2, 1, 0)))
    label = mm(placing, label.astype(F32).astype(BF16)).astype(BF16)
    if apart:
        l_refs[0][...] = label
    else:
        o_ref[:, 3 * BLOCK :] = label


def markers(ib_target, ib_owner, ib_block, ib_count, me, devices, ways, apart):
    capacity = ib_owner.shape[1]
    places = devices * MOST
    if apart:
        shapes = (jax.ShapeDtypeStruct((places, 3 * BLOCK), BF16),)
        shapes += (jax.ShapeDtypeStruct((places, BLOCK), BF16),)
    else:
        shapes = (jax.ShapeDtypeStruct((places, 4 * BLOCK), BF16),)
    return pl.pallas_call(
        functools.partial(marker_body, capacity, ways, apart),
        out_shape=shapes,
        in_specs=[pl.BlockSpec(memory_space=pltpu.SMEM)] * 2 + [pl.BlockSpec(memory_space=pltpu.VMEM)] * 4,
        out_specs=(pl.BlockSpec(memory_space=pltpu.VMEM),) * len(shapes),
        compiler_params=pltpu.CompilerParams(vmem_limit_bytes=VMEM),
        cost_estimate=cost(SHORT),
        name="markers",
    )(
        ib_count,
        me,
        ib_owner,
        ib_owner.reshape(capacity, 1),
        ib_block.reshape(capacity, 1),
        jnp.transpose(ib_target[0], (1, 0, 2)),
    )


def near_body(planes, comps, extra, near_columns, v_ref, dx_ref, dy_ref, mx_ref, my_ref, *rest):
    p_refs, (g_ref, band_ref, scale_ref) = rest[extra:-3], rest[-3:]
    rows, columns = v_ref.shape
    group = rows // (planes * comps)
    part = 512

    @pl.when(pl.program_id(0) == 0)
    def _():
        row = lax.broadcasted_iota(jnp.int32, (rows, planes), 0) % planes
        take = (row == lax.broadcasted_iota(jnp.int32, (rows, planes), 1)).astype(F32)
        scale_ref[...] = jnp.sum(take * my_ref[...], axis=1, keepdims=True)
        take = take.astype(BF16)
        spread = mm_nt(mm(take, dy_ref[...]).astype(BF16), take)
        one = lax.broadcasted_iota(jnp.int32, (rows, rows), 0) // planes
        other = lax.broadcasted_iota(jnp.int32, (rows, rows), 1) // planes
        band_ref[...] = jnp.where(one == other, spread, 0.0).astype(BF16)

    for j in range(columns // part):
        span = slice(j * part, (j + 1) * part)
        g_ref[:, span] = (mm_nt(v_ref[...], dx_ref[span, :]) * mx_ref[:, span]).astype(BF16)
    for j in range(columns // part):
        span = slice(j * part, (j + 1) * part)
        curv = mm_nt(g_ref[...], dx_ref[span, :]) * mx_ref[:, span]
        vel = v_ref[:, span]
        grad_y = (mm(band_ref[...], vel) * scale_ref[...]).astype(BF16)
        curv = curv + mm(band_ref[...], grad_y) * scale_ref[...]
        shape = (group, comps, planes, part)
        vel = vel.astype(F32).reshape(shape)
        grad_y = grad_y.astype(F32).reshape(shape)
        grad_x = g_ref[:, span].astype(F32).reshape(shape)
        curv = curv.reshape(shape)
        tendency = viscosity * curv - (vel[:, 0:1] * grad_x + vel[:, 1:2] * grad_y)
        at = j * part
        if at < near_columns:
            p_refs[0][:, :, :, span] = vel + time_step * tendency
        else:
            p_refs[-1][:, :, :, at - near_columns : at - near_columns + part] = vel + time_step * tendency


def near(lines, deriv_x, deriv_y, metric_x, metric_y, planes, comps, slab, near_columns, after):
    total, columns = lines.shape
    rows = GROUP * planes * comps
    far = columns - near_columns
    shapes = ((columns, near_columns), (far, far)) if near_columns else ((far, far),)
    return pl.pallas_call(
        functools.partial(near_body, planes, comps, len(after), near_columns),
        out_shape=tuple(jax.ShapeDtypeStruct((slab, comps, planes, n), F32) for n, _ in shapes),
        grid=(total // rows,),
        in_specs=[
            pl.BlockSpec((rows, columns), lambda i: (i, 0)),
            pl.BlockSpec(deriv_x.shape, lambda i: (0, 0), pipeline_mode=pl.Buffered(1)),
            pl.BlockSpec(deriv_y.shape, lambda i: (0, 0)),
            pl.BlockSpec((1, columns), lambda i: (0, 0)),
            pl.BlockSpec((1, planes), lambda i: (0, 0)),
        ]
        + [pl.BlockSpec(memory_space=pltpu.HBM)] * len(after),
        out_specs=tuple(pl.BlockSpec((GROUP, comps, planes, n), lambda i: (i, 0, 0, 0)) for _, n in shapes),
        scratch_shapes=[
            pltpu.VMEM((rows, columns), BF16),
            pltpu.VMEM((rows, rows), BF16),
            pltpu.VMEM((rows, 1), F32),
        ],
        compiler_params=pltpu.CompilerParams(vmem_limit_bytes=VMEM),
        cost_estimate=cost(SHORT),
        name="near",
    )(lines, deriv_x, deriv_y, metric_x, metric_y, *after)


def ready_markers(got_ref, s_ref, l_ref):
    lane = lax.broadcasted_iota(jnp.int32, (8, BLOCK), 1)
    pick = jnp.where(lane == 0, 128.0, jnp.where(lane < 3, 1.0, 0.0)).astype(BF16)
    slots = s_ref.shape[0]
    if len(got_ref.shape) == 4:
        values = [got_ref[:, :, c * MOST : (c + 1) * MOST, :] for c in range(4)]
    else:
        values = [got_ref[:, :, c * BLOCK : (c + 1) * BLOCK] for c in range(4)]
    values = [x.astype(F32).reshape(slots, BLOCK).astype(BF16) for x in values]
    l_ref[...] = mm_nt(pick, values[3]).astype(jnp.int32)
    for c in range(3):
        s_ref[:, c * BLOCK : (c + 1) * BLOCK] = values[c]
    s_ref[:, 3 * BLOCK :] = jnp.ones((slots, BLOCK), BF16)


def markers_spec(got, slab):
    if got.ndim == 4:
        rows = 4 * MOST
        block = (got.shape[0], got.shape[1], rows, got.shape[3])
        return pl.BlockSpec(block, lambda *_: (0, 0, 3 * slab // rows, 0)), got.shape[0] * got.shape[1] * MOST
    return pl.BlockSpec(got.shape, lambda *_: (0, 0, 0)), got.shape[0] * MOST


def settle(order_ref, taken, s_ref, l_ref, p_ref, o_ref, comps, wide, group, xblocks, first, at):
    slab = p_ref.shape[0]
    planes = p_ref.shape[2]
    lines = group * planes
    slots = s_ref.shape[0]
    label = l_ref[0:1, :]
    for g in range(slab // group):
        some = slice(g * group, (g + 1) * group)
        moved = mm(order_ref[...], taken(some).reshape(lines, comps * wide)) * time_step
        line = (g * lines + lax.broadcasted_iota(jnp.int32, (lines, slots), 0)) * xblocks + 1
        for b in range(wide // BLOCK):
            chosen = (line + (first + b) == label).astype(F32).astype(BF16)
            share = mm(chosen, s_ref[...])
            inverse = 1.0 / (1.0 + share[:, 3 * BLOCK :])
            cells = slice(at + b * BLOCK, at + (b + 1) * BLOCK)
            for c in range(comps):
                term = moved[:, c * wide + b * BLOCK : c * wide + (b + 1) * BLOCK]
                total = p_ref[some, c, :, cells].reshape(lines, BLOCK) + term + share[:, c * BLOCK : (c + 1) * BLOCK]
                o_ref[some, c, :, cells] = (total * inverse).reshape(group, planes, BLOCK)


def mark_body(planes, comps, group, xblocks, start, got_ref, p_ref, o_ref, i_ref, s_ref, l_ref):
    step = pl.program_id(0)

    @pl.when(step == 0)
    def _():
        ready_markers(got_ref, s_ref, l_ref)
        i_ref[...] = jnp.zeros_like(i_ref)

    blocks = p_ref.shape[3] // BLOCK
    lines = group * planes
    slots = s_ref.shape[0]
    for b in range(blocks):
        cells = slice(b * BLOCK, (b + 1) * BLOCK)
        for g in range(p_ref.shape[0] // group):
            some = slice(g * group, (g + 1) * group)
            line = (g * lines + lax.broadcasted_iota(jnp.int32, (lines, slots), 0)) * xblocks + 1
            chosen = (line + (start + step * blocks + b) == l_ref[0:1, :]).astype(F32).astype(BF16)
            share = mm(chosen, s_ref[...])
            inverse = 1.0 / (1.0 + share[:, 3 * BLOCK :])
            held = lax.broadcasted_iota(jnp.int32, (lines, BLOCK), 1) == step * blocks + b
            at = slice(g * lines, (g + 1) * lines)
            i_ref[at, :] = jnp.where(held, time_step * inverse, i_ref[at, :])
            for c in range(comps):
                total = p_ref[some, c, :, cells].reshape(lines, BLOCK) + share[:, c * BLOCK : (c + 1) * BLOCK]
                o_ref[some, c, :, cells] = (total * inverse).reshape(group, planes, BLOCK)


def mark(far, got, columns, group, after):
    slab, comps, planes, wide = far.shape
    step = 2 * BLOCK
    spec = pl.BlockSpec((slab, comps, planes, step), lambda i: (0, 0, 0, i))
    got_spec, slots = markers_spec(got, slab)

    def body(*refs):
        start = (columns - wide) // BLOCK
        mark_body(planes, comps, group, columns // BLOCK, start, *refs[:2], *refs[2 + len(after) :])

    return pl.pallas_call(
        body,
        out_shape=(
            jax.ShapeDtypeStruct(far.shape, F32),
            jax.ShapeDtypeStruct((slab * planes, BLOCK), F32),
        ),
        grid=(wide // step,),
        in_specs=[got_spec, spec] + [pl.BlockSpec(memory_space=pltpu.HBM)] * len(after),
        out_specs=(spec, pl.BlockSpec((slab * planes, BLOCK), lambda i: (0, 0))),
        scratch_shapes=[pltpu.VMEM((slots, 4 * BLOCK), BF16), pltpu.VMEM((8, slots), jnp.int32)],
        compiler_params=pltpu.CompilerParams(vmem_limit_bytes=ROOM),
        cost_estimate=cost(SHORT),
        name="mark",
    )(got, far, *after)


def last_body(planes, comps, count, extra, order_ref, *rest):
    r_refs, (i_ref, p_ref), o_ref = rest[:count], rest[count : count + 2], rest[count + 2 + extra]
    group = p_ref.shape[0]
    groups = r_refs[0].shape[1]
    lines = group * planes
    for q in range(count):
        for xg in range(groups):
            at = (q * groups + xg) * BLOCK
            cells = slice(at, at + BLOCK)
            moved = mm(order_ref[...], r_refs[q][:, xg].reshape(lines, comps * BLOCK))
            weight = i_ref[:, q * groups + xg : q * groups + xg + 1]
            for c in range(comps):
                term = (moved[:, c * BLOCK : (c + 1) * BLOCK] * weight).reshape(group, planes, BLOCK)
                o_ref[:, c, :, cells] = p_ref[:, c, :, cells] + term


def last(field, far, weight, returned, order):
    slab, comps, planes, wide = far.shape
    groups = returned.shape[1]
    count = wide // (groups * BLOCK)
    rows = order.shape[0] // planes
    steps = slab // rows
    columns = wide if field is None else field.shape[3]
    skip = columns // wide - 1
    held = () if field is None else (field,)
    return pl.pallas_call(
        functools.partial(last_body, planes, comps, count, len(held)),
        out_shape=jax.ShapeDtypeStruct((slab, comps, planes, columns), F32),
        grid=(steps,),
        in_specs=[pl.BlockSpec(order.shape, lambda i: (0, 0))]
        + [
            pl.BlockSpec((planes, groups, rows, comps * BLOCK), lambda i, q=q: (0, 0, q * steps + i, 0))
            for q in range(count)
        ]
        + [
            pl.BlockSpec((rows * planes, BLOCK), lambda i: (i, 0)),
            pl.BlockSpec((rows, comps, planes, wide), lambda i: (i, 0, 0, 0)),
        ]
        + [pl.BlockSpec(memory_space=pltpu.HBM)] * len(held),
        out_specs=pl.BlockSpec((rows, comps, planes, wide), lambda i: (i, 0, 0, skip)),
        input_output_aliases={3 + count: 0} if held else {},
        compiler_params=pltpu.CompilerParams(vmem_limit_bytes=ROOM),
        cost_estimate=cost(SHORT),
        name="last",
    )(order, *([returned] * count), weight, far, *held)


def last_apart_body(comps, group, xblocks, start, ways, me_ref, order_ref, got_ref, own_ref, *rest):
    pieces, p_ref = rest[: ways - 1], rest[ways - 1]
    o_ref, s_ref, l_ref, t_ref = rest[-4:]
    step = pl.program_id(0)

    @pl.when(step == 0)
    def _():
        ready_markers(got_ref, s_ref, l_ref)
        t_ref[...] = own_ref[:, 0]

    for k in range(1, ways):

        @pl.when(step == k)
        def _(k=k):
            t_ref[...] = pieces[k - 1][...]

    settle(
        order_ref,
        lambda some: t_ref[:, some, :],
        s_ref,
        l_ref,
        p_ref,
        o_ref,
        comps,
        BLOCK,
        group,
        xblocks,
        start + (me_ref[0] ^ step),
        0,
    )


def last_apart(field, own, pieces, got, order, me, chunk, group, after):
    slab, comps, planes, columns = field.shape
    ways = own.shape[1]
    spec = pl.BlockSpec((slab, comps, planes, BLOCK), lambda i, m: (0, 0, 0, chunk * ways + (m[0] ^ i)))
    whole = pl.BlockSpec((planes, slab, comps * BLOCK), lambda i, m: (0, 0, 0))
    got_spec, slots = markers_spec(got, slab)
    return pl.pallas_call(
        functools.partial(last_apart_body, comps, group, columns // BLOCK, chunk * ways, ways),
        out_shape=jax.ShapeDtypeStruct(field.shape, F32),
        grid_spec=pltpu.PrefetchScalarGridSpec(
            num_scalar_prefetch=1,
            grid=(ways,),
            in_specs=[
                pl.BlockSpec(order.shape, lambda i, m: (0, 0)),
                got_spec,
                pl.BlockSpec((planes, 1, slab, comps * BLOCK), lambda i, m: (0, 0, chunk, 0)),
            ]
            + [whole] * (ways - 1)
            + [spec]
            + [pl.BlockSpec(memory_space=pltpu.HBM)] * len(after),
            out_specs=spec,
            scratch_shapes=[
                pltpu.VMEM((slots, 4 * BLOCK), BF16),
                pltpu.VMEM((8, slots), jnp.int32),
                pltpu.VMEM((planes, slab, comps * BLOCK), BF16),
            ],
        ),
        input_output_aliases={4 + ways - 1: 0},
        compiler_params=pltpu.CompilerParams(vmem_limit_bytes=VMEM),
        cost_estimate=cost(LONG),
        name="last_apart",
    )(me, order, got, own, *pieces, field, *after)


def come_body(count, *refs):
    refs[count][...] = jnp.zeros_like(refs[count])


def come(pieces):
    return pl.pallas_call(
        functools.partial(come_body, len(pieces)),
        out_shape=jax.ShapeDtypeStruct((8, BLOCK), F32),
        in_specs=[pl.BlockSpec(memory_space=pltpu.HBM)] * len(pieces),
        out_specs=pl.BlockSpec(memory_space=pltpu.VMEM),
        cost_estimate=cost(LONG),
        name="come",
    )(*pieces)


def across(pieces):
    ways = lax.axis_size("col")
    return tuple(
        lax.ppermute(piece, "col", [(c, c ^ k) for c in range(ways)]) for k, piece in enumerate(pieces, 1)
    )


def along(x):
    return lax.all_to_all(x, "row", split_axis=0, concat_axis=0, tiled=True)


def exchange(x):
    return lax.all_to_all(x, AXES, split_axis=0, concat_axis=0, tiled=True)


def local(
    velocity,
    deriv_x,
    deriv_y,
    deriv_z,
    metric_x,
    metric_y,
    metric_z,
    ib_target,
    ib_owner,
    ib_block,
    ib_count,
):
    slab, planes, comps, columns = velocity.shape
    row_count, ways = lax.axis_size("row"), lax.axis_size("col")
    devices = row_count * ways
    groups = devices // planes
    group = min(32, slab)
    chunks = columns // (groups * BLOCK)
    me = lax.axis_index("col").astype(jnp.int32).reshape(1)
    lines = jnp.transpose(velocity, (0, 2, 1, 3)).reshape(slab * comps * planes, columns)
    order = jnp.asarray(pack_order(planes, comps, GROUP), BF16)
    quick = jnp.asarray(pack_order(planes, comps, GROUP // 2), BF16)
    back = jnp.asarray(unpack_order(planes, group), BF16)
    small = jnp.asarray(unpack_order(planes, LAST), BF16)
    metric_col = metric_z[:, None]
    apart = row_count == planes and chunks == QUARTERS and slab == QUARTERS * GROUP
    marked, *labels = markers(ib_target, ib_owner, ib_block, ib_count, me, devices, ways, apart)
    at_once = 2 if apart else chunks
    near_columns = columns // 2 if apart else 0
    first = pack(lines, quick, at_once, planes, comps, groups, slab)
    block = (devices,) + first.shape[2:]
    arrived = exchange(first.reshape(block)).reshape((row_count, ways) + first.shape[2:])
    *fields, far = near(
        lines, deriv_x, deriv_y, metric_x[None, :], metric_y[None, :], planes, comps, slab, near_columns, (first,)
    )

    if not apart:
        got = exchange(marked.reshape(devices, MOST, 4 * BLOCK))
        terms = depth(arrived, me, deriv_z, metric_col, at_once, slab, False, False, (far,))
        home = exchange(terms.reshape(block)).reshape(first.shape)
        far, weight = mark(far, got, columns, group, ())
        return jnp.transpose(last(None, far, weight, home, small), (0, 2, 1, 3))

    def outward(k, after, marked=None):
        return pack_apart(lines, order, me, k, planes, comps, ways, slab, after, marked)

    (field,) = fields
    marked = (marked.reshape(ways, planes, MOST, comps * BLOCK), labels[0].reshape(ways, planes, MOST, BLOCK))
    sent3 = outward(3, (field,))
    sent2 = outward(2, (sent3[0],), marked)
    later2, later3 = lax.optimization_barrier((sent2[EARLY:], sent3[EARLY:], arrived))[:2]
    come2 = across(tuple(sent2[1:EARLY]) + tuple(later2))
    come3 = across(tuple(sent3[1:EARLY]) + tuple(later3))
    terms = depth(arrived, me, deriv_z, metric_col, 2, slab, False, True, (sent2[0],))
    home = along(terms)
    joined2 = join((sent2[0],) + come2, (terms,))
    split0 = split(home, 0, slab, (joined2,))
    back0 = across(split0)
    split1 = split(home, 1, slab, (split0[0],))
    back1 = across(split1)
    got = full2 = along(joined2)
    joined3 = join((sent3[0],) + come3, (split1[0],))
    full3 = along(joined3)
    terms = depth(full2, me, deriv_z, metric_col, 1, slab, True, False, (joined3,), 0, 2)
    terms = depth(full3, me, deriv_z, metric_col, 1, slab, True, False, (come(back0),), 1, 2, (terms,))
    home_all = exchange(terms.reshape(block)).reshape(first.shape)
    field = last_apart(field, home, back0, got, back, me, 0, group, (terms,))
    field = last_apart(field, home, back1, got, back, me, 1, group, ())
    far, weight = mark(far, got, columns, group, (field,))
    return jnp.transpose(last(field, far, weight, home_all, small), (0, 2, 1, 3))


def solution(mesh):
    in_specs = (
        P(AXES, None, None, None),
        P(),
        P(),
        P(),
        P(),
        P(),
        P(),
        P(AXES, None, None, None),
        P(AXES, None),
        P(AXES, None),
        P(AXES),
    )
    out_specs = P(AXES, None, None, None)
    return jax.shard_map(local, mesh=mesh, in_specs=in_specs, out_specs=out_specs, check_vma=False)
```

```python
import functools

import jax
import jax.numpy as jnp
import numpy as np
from jax import lax
from jax.experimental import pallas as pl
from jax.experimental.pallas import tpu as pltpu
from jax.sharding import PartitionSpec as P

BLOCK = 128
MOST = 8
GROUP = 16
QUARTERS = 4
VMEM = 60 << 20
ROOM = 60 << 20
LAST = 16
SHORT = 1
EARLY = 2
PACK = 4
LONG = 10**12

viscosity = 0.4
time_step = 0.2

F32 = jnp.float32
BF16 = jnp.bfloat16
AXES = ("row", "col")


def cost(flops):
    return pl.CostEstimate(flops=flops, bytes_accessed=1, transcendentals=0)


def mm(a, b):
    return lax.dot_general(a, b, (((1,), (0,)), ((), ())), preferred_element_type=F32)


def mm_nt(a, b):
    return lax.dot_general(a, b, (((1,), (1,)), ((), ())), preferred_element_type=F32)


def pack_order(planes, comps, group):
    rows = group * planes * comps
    table = np.zeros((rows, rows), np.float32)
    for y in range(planes):
        for c in range(comps):
            for z in range(group):
                table[(y * comps + c) * group + z, (z * comps + c) * planes + y] = 1
    return table


def unpack_order(planes, group):
    rows = group * planes
    table = np.zeros((rows, rows), np.float32)
    for y in range(planes):
        for z in range(group):
            table[z * planes + y, y * group + z] = 1
    return table


def place_rows(o_ref, moved, planes, comps, wide, at_rows, spot):
    for y in range(planes):
        for c in range(comps):
            group = moved.shape[0] // (planes * comps)
            at = (y * comps + c) * group
            o_ref[y, at_rows, c * wide : (c + 1) * wide] = moved[at : at + group, spot]


def pack_body(planes, comps, wide, order_ref, v_ref, o_ref):
    lanes = v_ref.shape[1]
    rows = order_ref.shape[0]
    group = rows // (planes * comps)
    for g in range(v_ref.shape[0] // rows):
        moved = mm(order_ref[...], v_ref[g * rows : (g + 1) * rows, :]).astype(BF16)
        for xg in range(lanes // wide):
            place_rows(
                o_ref.at[:, xg],
                moved,
                planes,
                comps,
                wide,
                slice(g * group, (g + 1) * group),
                slice(xg * wide, (xg + 1) * wide),
            )


def pack(lines, order, count, planes, comps, groups, slab):
    many = PACK
    step = many * BLOCK
    steps = groups // many
    return pl.pallas_call(
        functools.partial(pack_body, planes, comps, BLOCK),
        out_shape=jax.ShapeDtypeStruct((planes, groups, count * slab, comps * BLOCK), BF16),
        grid=(count, steps),
        in_specs=[
            pl.BlockSpec(order.shape, lambda q, i: (0, 0)),
            pl.BlockSpec((lines.shape[0], step), lambda q, i: (0, q * steps + i)),
        ],
        out_specs=pl.BlockSpec((planes, many, slab, comps * BLOCK), lambda q, i: (0, i, q, 0)),
        compiler_params=pltpu.CompilerParams(vmem_limit_bytes=VMEM),
        cost_estimate=cost(SHORT),
        name="pack",
    )(order, lines)


def pack_apart_body(planes, comps, ways, given, extra, me_ref, order_ref, *rest):
    v_refs, o_refs = rest[:ways], rest[ways + given + extra :]
    rows = order_ref.shape[0]
    groups = v_refs[0].shape[0] // rows
    slab = groups * GROUP
    for g in range(groups):
        whole = jnp.concatenate([v_ref[g * rows : (g + 1) * rows, :] for v_ref in v_refs], axis=1)
        moved = mm(order_ref[...], whole).astype(BF16)
        spot = slice(g * GROUP, (g + 1) * GROUP)
        for k in range(ways):
            cells = slice(k * BLOCK, (k + 1) * BLOCK)
            if not given:
                place_rows(o_refs[k], moved, planes, comps, BLOCK, spot, cells)
                continue
            for y in range(planes):
                for c in range(comps):
                    at = (y * comps + c) * GROUP
                    to = c * slab + g * GROUP
                    o_refs[k][y, to : to + GROUP, :] = moved[at : at + GROUP, cells]
    if given:
        for k in range(ways):
            at = comps * slab
            for c in range(comps):
                o_refs[k][:, at + c * MOST : at + (c + 1) * MOST, :] = rest[ways][
                    k, :, :, c * BLOCK : (c + 1) * BLOCK
                ]
            o_refs[k][:, at + comps * MOST :, :] = rest[ways + 1][k]


def pack_apart(lines, order, me, chunk, planes, comps, ways, slab, after, marked=None):
    total = lines.shape[0]
    given = () if marked is None else marked
    shape = (planes, comps * slab + (comps + 1) * MOST, BLOCK) if given else (planes, slab, comps * BLOCK)
    return pl.pallas_call(
        functools.partial(pack_apart_body, planes, comps, ways, len(given), len(after)),
        out_shape=(jax.ShapeDtypeStruct(shape, BF16),) * ways,
        grid_spec=pltpu.PrefetchScalarGridSpec(
            num_scalar_prefetch=1,
            grid=(1,),
            in_specs=[pl.BlockSpec(order.shape, lambda i, m: (0, 0))]
            + [pl.BlockSpec((total, BLOCK), lambda i, m, k=k: (0, chunk * ways + (m[0] ^ k))) for k in range(ways)]
            + [pl.BlockSpec(x.shape, lambda i, m: (0, 0, 0, 0)) for x in given]
            + [pl.BlockSpec(memory_space=pltpu.HBM)] * len(after),
            out_specs=(pl.BlockSpec(shape, lambda i, m: (0, 0, 0)),) * ways,
        ),
        compiler_params=pltpu.CompilerParams(vmem_limit_bytes=VMEM),
        cost_estimate=cost(SHORT),
        name="pack_apart",
    )(me, order, *([lines] * ways), *given, *after)


def join_body(ways, *refs):
    for k in range(ways):
        refs[-1][:, k] = refs[k][...]


def join(pieces, after):
    ways = len(pieces)
    planes, height, cols = pieces[0].shape
    half = planes // 2
    return pl.pallas_call(
        functools.partial(join_body, ways),
        out_shape=jax.ShapeDtypeStruct((planes, ways, height, cols), BF16),
        grid=(2,),
        in_specs=[pl.BlockSpec((half, height, cols), lambda i: (i, 0, 0))] * ways
        + [pl.BlockSpec(memory_space=pltpu.HBM)] * len(after),
        out_specs=pl.BlockSpec((half, ways, height, cols), lambda i: (i, 0, 0, 0)),
        compiler_params=pltpu.CompilerParams(vmem_limit_bytes=VMEM),
        cost_estimate=cost(LONG),
        name="join",
    )(*pieces, *after)


def split_body(ways, count, x_ref, *rest):
    for k in range(1, ways):
        rest[count + k - 1][...] = x_ref[:, k]


def split(x, quarter, slab, after):
    planes, ways, _, cols = x.shape
    half = planes // 2
    return pl.pallas_call(
        functools.partial(split_body, ways, len(after)),
        out_shape=(jax.ShapeDtypeStruct((planes, slab, cols), BF16),) * (ways - 1),
        grid=(2,),
        in_specs=[pl.BlockSpec((half, ways, slab, cols), lambda i: (i, 0, quarter, 0))]
        + [pl.BlockSpec(memory_space=pltpu.HBM)] * len(after),
        out_specs=(pl.BlockSpec((half, slab, cols), lambda i: (i, 0, 0)),) * (ways - 1),
        compiler_params=pltpu.CompilerParams(vmem_limit_bytes=VMEM),
        cost_estimate=cost(SHORT),
        name="split",
    )(x, *after)


def depth_body(count, slab, block, extra, near_in, near_out, me_ref, x_ref, d_ref, m_ref, *rest):
    o_ref, s_ref, g_ref = rest[extra:]
    tall, ways, height, cols = x_ref.shape
    stacked = cols == BLOCK
    cols = 3 * BLOCK
    wide = cols // 3
    phase = pl.program_id(0)
    step = pl.program_id(1)
    spot = pl.ds(pl.multiple_of(step * block, block), block)
    me = me_ref[0]

    @pl.when((phase == 0) & (step == 0))
    def _():
        for r in range(tall):
            for k in range(ways):
                to = pl.multiple_of((r * ways + (me ^ k if near_in else k)) * slab, slab)
                for q in range(1 if stacked else count):
                    s_ref[pl.ds(to, slab), q * cols : (q + 1) * cols] = (
                        jnp.concatenate([x_ref[r, k, c * slab : (c + 1) * slab] for c in range(3)], axis=1)
                        if stacked
                        else x_ref[r, k, q * slab : (q + 1) * slab]
                    )

    @pl.when(phase == 0)
    def _():
        g_ref[spot, :] = (mm(d_ref[...], s_ref[...]) * m_ref[spot, :]).astype(BF16)

    @pl.when(phase == 1)
    def _():
        curv = mm(d_ref[...], g_ref[...]) * m_ref[spot, :]
        grad = g_ref[spot, :].astype(F32)
        each = block // slab
        for q in range(count):
            upward = s_ref[spot, q * cols + 2 * wide : q * cols + 3 * wide].astype(F32)
            for c in range(3):
                part = slice(q * cols + c * wide, q * cols + (c + 1) * wide)
                term = (viscosity * curv[:, part] - upward * grad[:, part]).astype(BF16)
                for n in range(each):
                    r = step * (each // ways) + n // ways
                    k = me ^ (n % ways) if near_out else n % ways
                    o_ref[r, k, q * slab : (q + 1) * slab, c * wide : (c + 1) * wide] = term[
                        n * slab : (n + 1) * slab, :
                    ]


def depth(x, me, deriv_z, metric_z, count, slab, near_in, near_out, after, place=0, total=None, held=()):
    tall, ways, _, cols = x.shape
    given = (tall, ways, count * slab if cols > BLOCK else 3 * slab, cols)
    cols = 3 * BLOCK
    shape = (tall, ways, count * slab, cols)
    extra = tuple(held) + tuple(after)
    height = deriv_z.shape[0]
    block = 512
    return pl.pallas_call(
        functools.partial(depth_body, count, slab, block, len(extra), near_in, near_out),
        out_shape=jax.ShapeDtypeStruct((tall, ways, (total or count) * slab, cols), BF16),
        grid_spec=pltpu.PrefetchScalarGridSpec(
            num_scalar_prefetch=1,
            grid=(2, height // block),
            in_specs=[
                pl.BlockSpec(given, lambda p, i, m: (0, 0, 0, 0)),
                pl.BlockSpec((block, height), lambda p, i, m: (i, 0)),
                pl.BlockSpec((height, 1), lambda p, i, m: (0, 0)),
            ]
            + [pl.BlockSpec(memory_space=pltpu.HBM)] * len(extra),
            out_specs=pl.BlockSpec(shape, lambda p, i, m: (0, 0, place, 0)),
            scratch_shapes=[pltpu.VMEM((height, count * cols), BF16), pltpu.VMEM((height, count * cols), BF16)],
        ),
        input_output_aliases={4: 0} if held else {},
        compiler_params=pltpu.CompilerParams(vmem_limit_bytes=VMEM),
        cost_estimate=cost(SHORT),
        name="depth",
    )(me, x, deriv_z, metric_z, *extra)


def marker_body(capacity, ways, apart, count_ref, me_ref, owner_row, owner_col, block_col, t_ref, o_ref, *l_refs):
    earlier = lax.broadcasted_iota(jnp.int32, (capacity, capacity), 0)
    later = lax.broadcasted_iota(jnp.int32, (capacity, capacity), 1)
    same = (owner_col[...] == owner_row[...]) & (earlier < later)
    position = jnp.sum(same.astype(jnp.int32), axis=0, keepdims=True)
    slot = lax.broadcasted_iota(jnp.int32, (1, capacity), 1)
    owner = owner_row[...]
    places = o_ref.shape[0]
    if apart:
        owner = ((owner % ways) ^ me_ref[0]) * (places // (ways * MOST)) + owner // ways
    slotted = jnp.where(slot < count_ref[0], owner * MOST + position, places)
    placing = (lax.broadcasted_iota(jnp.int32, (places, capacity), 0) == slotted).astype(F32).astype(BF16)
    for c in range(3):
        o_ref[:, c * BLOCK : (c + 1) * BLOCK] = mm(placing, t_ref[c]).astype(BF16)
    lane = lax.broadcasted_iota(jnp.int32, (capacity, BLOCK), 1)
    high = block_col[...] // 128
    low = block_col[...] - high * 128
    label = jnp.where(lane == 0, high, jnp.where(lane == 1, low, jnp.where(lane == 2, 1, 0)))
    label = mm(placing, label.astype(F32).astype(BF16)).astype(BF16)
    if apart:
        l_refs[0][...] = label
    else:
        o_ref[:, 3 * BLOCK :] = label


def markers(ib_target, ib_owner, ib_block, ib_count, me, devices, ways, apart):
    capacity = ib_owner.shape[1]
    places = devices * MOST
    if apart:
        shapes = (jax.ShapeDtypeStruct((places, 3 * BLOCK), BF16),)
        shapes += (jax.ShapeDtypeStruct((places, BLOCK), BF16),)
    else:
        shapes = (jax.ShapeDtypeStruct((places, 4 * BLOCK), BF16),)
    return pl.pallas_call(
        functools.partial(marker_body, capacity, ways, apart),
        out_shape=shapes,
        in_specs=[pl.BlockSpec(memory_space=pltpu.SMEM)] * 2 + [pl.BlockSpec(memory_space=pltpu.VMEM)] * 4,
        out_specs=(pl.BlockSpec(memory_space=pltpu.VMEM),) * len(shapes),
        compiler_params=pltpu.CompilerParams(vmem_limit_bytes=VMEM),
        cost_estimate=cost(SHORT),
        name="markers",
    )(
        ib_count,
        me,
        ib_owner,
        ib_owner.reshape(capacity, 1),
        ib_block.reshape(capacity, 1),
        jnp.transpose(ib_target[0], (1, 0, 2)),
    )


def near_body(planes, comps, extra, near_columns, v_ref, dx_ref, dy_ref, mx_ref, my_ref, *rest):
    p_refs, (g_ref, band_ref, scale_ref) = rest[extra:-3], rest[-3:]
    rows, columns = v_ref.shape
    group = rows // (planes * comps)
    part = 512

    @pl.when(pl.program_id(0) == 0)
    def _():
        row = lax.broadcasted_iota(jnp.int32, (rows, planes), 0) % planes
        take = (row == lax.broadcasted_iota(jnp.int32, (rows, planes), 1)).astype(F32)
        scale_ref[...] = jnp.sum(take * my_ref[...], axis=1, keepdims=True)
        take = take.astype(BF16)
        spread = mm_nt(mm(take, dy_ref[...]).astype(BF16), take)
        one = lax.broadcasted_iota(jnp.int32, (rows, rows), 0) // planes
        other = lax.broadcasted_iota(jnp.int32, (rows, rows), 1) // planes
        band_ref[...] = jnp.where(one == other, spread, 0.0).astype(BF16)

    for j in range(columns // part):
        span = slice(j * part, (j + 1) * part)
        g_ref[:, span] = (mm_nt(v_ref[...], dx_ref[span, :]) * mx_ref[:, span]).astype(BF16)
    for j in range(columns // part):
        span = slice(j * part, (j + 1) * part)
        curv = mm_nt(g_ref[...], dx_ref[span, :]) * mx_ref[:, span]
        vel = v_ref[:, span]
        grad_y = (mm(band_ref[...], vel) * scale_ref[...]).astype(BF16)
        curv = curv + mm(band_ref[...], grad_y) * scale_ref[...]
        shape = (group, comps, planes, part)
        vel = vel.astype(F32).reshape(shape)
        grad_y = grad_y.astype(F32).reshape(shape)
        grad_x = g_ref[:, span].astype(F32).reshape(shape)
        curv = curv.reshape(shape)
        tendency = viscosity * curv - (vel[:, 0:1] * grad_x + vel[:, 1:2] * grad_y)
        at = j * part
        if at < near_columns:
            p_refs[0][:, :, :, span] = vel + time_step * tendency
        else:
            p_refs[-1][:, :, :, at - near_columns : at - near_columns + part] = vel + time_step * tendency


def near(lines, deriv_x, deriv_y, metric_x, metric_y, planes, comps, slab, near_columns, after):
    total, columns = lines.shape
    rows = GROUP * planes * comps
    far = columns - near_columns
    shapes = ((columns, near_columns), (far, far)) if near_columns else ((far, far),)
    return pl.pallas_call(
        functools.partial(near_body, planes, comps, len(after), near_columns),
        out_shape=tuple(jax.ShapeDtypeStruct((slab, comps, planes, n), F32) for n, _ in shapes),
        grid=(total // rows,),
        in_specs=[
            pl.BlockSpec((rows, columns), lambda i: (i, 0)),
            pl.BlockSpec(deriv_x.shape, lambda i: (0, 0), pipeline_mode=pl.Buffered(1)),
            pl.BlockSpec(deriv_y.shape, lambda i: (0, 0)),
            pl.BlockSpec((1, columns), lambda i: (0, 0)),
            pl.BlockSpec((1, planes), lambda i: (0, 0)),
        ]
        + [pl.BlockSpec(memory_space=pltpu.HBM)] * len(after),
        out_specs=tuple(pl.BlockSpec((GROUP, comps, planes, n), lambda i: (i, 0, 0, 0)) for _, n in shapes),
        scratch_shapes=[
            pltpu.VMEM((rows, columns), BF16),
            pltpu.VMEM((rows, rows), BF16),
            pltpu.VMEM((rows, 1), F32),
        ],
        compiler_params=pltpu.CompilerParams(vmem_limit_bytes=VMEM),
        cost_estimate=cost(SHORT),
        name="near",
    )(lines, deriv_x, deriv_y, metric_x, metric_y, *after)


def ready_markers(got_ref, s_ref, l_ref):
    lane = lax.broadcasted_iota(jnp.int32, (8, BLOCK), 1)
    pick = jnp.where(lane == 0, 128.0, jnp.where(lane < 3, 1.0, 0.0)).astype(BF16)
    slots = s_ref.shape[0]
    if len(got_ref.shape) == 4:
        values = [got_ref[:, :, c * MOST : (c + 1) * MOST, :] for c in range(4)]
    else:
        values = [got_ref[:, :, c * BLOCK : (c + 1) * BLOCK] for c in range(4)]
    values = [x.astype(F32).reshape(slots, BLOCK).astype(BF16) for x in values]
    l_ref[...] = mm_nt(pick, values[3]).astype(jnp.int32)
    for c in range(3):
        s_ref[:, c * BLOCK : (c + 1) * BLOCK] = values[c]
    s_ref[:, 3 * BLOCK :] = jnp.ones((slots, BLOCK), BF16)


def markers_spec(got, slab):
    if got.ndim == 4:
        rows = 4 * MOST
        block = (got.shape[0], got.shape[1], rows, got.shape[3])
        return pl.BlockSpec(block, lambda *_: (0, 0, 3 * slab // rows, 0)), got.shape[0] * got.shape[1] * MOST
    return pl.BlockSpec(got.shape, lambda *_: (0, 0, 0)), got.shape[0] * MOST


def settle(order_ref, taken, s_ref, l_ref, p_ref, o_ref, comps, wide, group, xblocks, first, at):
    slab = p_ref.shape[0]
    planes = p_ref.shape[2]
    lines = group * planes
    slots = s_ref.shape[0]
    label = l_ref[0:1, :]
    for g in range(slab // group):
        some = slice(g * group, (g + 1) * group)
        moved = mm(order_ref[...], taken(some).reshape(lines, comps * wide)) * time_step
        line = (g * lines + lax.broadcasted_iota(jnp.int32, (lines, slots), 0)) * xblocks + 1
        for b in range(wide // BLOCK):
            chosen = (line + (first + b) == label).astype(F32).astype(BF16)
            share = mm(chosen, s_ref[...])
            inverse = 1.0 / (1.0 + share[:, 3 * BLOCK :])
            cells = slice(at + b * BLOCK, at + (b + 1) * BLOCK)
            for c in range(comps):
                term = moved[:, c * wide + b * BLOCK : c * wide + (b + 1) * BLOCK]
                total = p_ref[some, c, :, cells].reshape(lines, BLOCK) + term + share[:, c * BLOCK : (c + 1) * BLOCK]
                o_ref[some, c, :, cells] = (total * inverse).reshape(group, planes, BLOCK)


def mark_body(planes, comps, group, xblocks, start, got_ref, p_ref, o_ref, i_ref, s_ref, l_ref):
    step = pl.program_id(0)

    @pl.when(step == 0)
    def _():
        ready_markers(got_ref, s_ref, l_ref)
        i_ref[...] = jnp.zeros_like(i_ref)

    blocks = p_ref.shape[3] // BLOCK
    lines = group * planes
    slots = s_ref.shape[0]
    for b in range(blocks):
        cells = slice(b * BLOCK, (b + 1) * BLOCK)
        for g in range(p_ref.shape[0] // group):
            some = slice(g * group, (g + 1) * group)
            line = (g * lines + lax.broadcasted_iota(jnp.int32, (lines, slots), 0)) * xblocks + 1
            chosen = (line + (start + step * blocks + b) == l_ref[0:1, :]).astype(F32).astype(BF16)
            share = mm(chosen, s_ref[...])
            inverse = 1.0 / (1.0 + share[:, 3 * BLOCK :])
            held = lax.broadcasted_iota(jnp.int32, (lines, BLOCK), 1) == step * blocks + b
            at = slice(g * lines, (g + 1) * lines)
            i_ref[at, :] = jnp.where(held, time_step * inverse, i_ref[at, :])
            for c in range(comps):
                total = p_ref[some, c, :, cells].reshape(lines, BLOCK) + share[:, c * BLOCK : (c + 1) * BLOCK]
                o_ref[some, c, :, cells] = (total * inverse).reshape(group, planes, BLOCK)


def mark(far, got, columns, group, after):
    slab, comps, planes, wide = far.shape
    step = 2 * BLOCK
    spec = pl.BlockSpec((slab, comps, planes, step), lambda i: (0, 0, 0, i))
    got_spec, slots = markers_spec(got, slab)

    def body(*refs):
        start = (columns - wide) // BLOCK
        mark_body(planes, comps, group, columns // BLOCK, start, *refs[:2], *refs[2 + len(after) :])

    return pl.pallas_call(
        body,
        out_shape=(
            jax.ShapeDtypeStruct(far.shape, F32),
            jax.ShapeDtypeStruct((slab * planes, BLOCK), F32),
        ),
        grid=(wide // step,),
        in_specs=[got_spec, spec] + [pl.BlockSpec(memory_space=pltpu.HBM)] * len(after),
        out_specs=(spec, pl.BlockSpec((slab * planes, BLOCK), lambda i: (0, 0))),
        scratch_shapes=[pltpu.VMEM((slots, 4 * BLOCK), BF16), pltpu.VMEM((8, slots), jnp.int32)],
        compiler_params=pltpu.CompilerParams(vmem_limit_bytes=ROOM),
        cost_estimate=cost(SHORT),
        name="mark",
    )(got, far, *after)


def last_body(planes, comps, count, extra, order_ref, *rest):
    r_refs, (i_ref, p_ref), o_ref = rest[:count], rest[count : count + 2], rest[count + 2 + extra]
    group = p_ref.shape[0]
    groups = r_refs[0].shape[1]
    lines = group * planes
    for q in range(count):
        for xg in range(groups):
            at = (q * groups + xg) * BLOCK
            cells = slice(at, at + BLOCK)
            moved = mm(order_ref[...], r_refs[q][:, xg].reshape(lines, comps * BLOCK))
            weight = i_ref[:, q * groups + xg : q * groups + xg + 1]
            for c in range(comps):
                term = (moved[:, c * BLOCK : (c + 1) * BLOCK] * weight).reshape(group, planes, BLOCK)
                o_ref[:, c, :, cells] = p_ref[:, c, :, cells] + term


def last(field, far, weight, returned, order):
    slab, comps, planes, wide = far.shape
    groups = returned.shape[1]
    count = wide // (groups * BLOCK)
    rows = order.shape[0] // planes
    steps = slab // rows
    columns = wide if field is None else field.shape[3]
    skip = columns // wide - 1
    held = () if field is None else (field,)
    return pl.pallas_call(
        functools.partial(last_body, planes, comps, count, len(held)),
        out_shape=jax.ShapeDtypeStruct((slab, comps, planes, columns), F32),
        grid=(steps,),
        in_specs=[pl.BlockSpec(order.shape, lambda i: (0, 0))]
        + [
            pl.BlockSpec((planes, groups, rows, comps * BLOCK), lambda i, q=q: (0, 0, q * steps + i, 0))
            for q in range(count)
        ]
        + [
            pl.BlockSpec((rows * planes, BLOCK), lambda i: (i, 0)),
            pl.BlockSpec((rows, comps, planes, wide), lambda i: (i, 0, 0, 0)),
        ]
        + [pl.BlockSpec(memory_space=pltpu.HBM)] * len(held),
        out_specs=pl.BlockSpec((rows, comps, planes, wide), lambda i: (i, 0, 0, skip)),
        input_output_aliases={3 + count: 0} if held else {},
        compiler_params=pltpu.CompilerParams(vmem_limit_bytes=ROOM),
        cost_estimate=cost(SHORT),
        name="last",
    )(order, *([returned] * count), weight, far, *held)


def last_apart_body(comps, group, xblocks, start, ways, me_ref, order_ref, got_ref, own_ref, *rest):
    pieces, p_ref = rest[: ways - 1], rest[ways - 1]
    o_ref, s_ref, l_ref, t_ref = rest[-4:]
    step = pl.program_id(0)

    @pl.when(step == 0)
    def _():
        ready_markers(got_ref, s_ref, l_ref)
        t_ref[...] = own_ref[:, 0]

    for k in range(1, ways):

        @pl.when(step == k)
        def _(k=k):
            t_ref[...] = pieces[k - 1][...]

    settle(
        order_ref,
        lambda some: t_ref[:, some, :],
        s_ref,
        l_ref,
        p_ref,
        o_ref,
        comps,
        BLOCK,
        group,
        xblocks,
        start + (me_ref[0] ^ step),
        0,
    )


def last_apart(field, own, pieces, got, order, me, chunk, group, after):
    slab, comps, planes, columns = field.shape
    ways = own.shape[1]
    spec = pl.BlockSpec((slab, comps, planes, BLOCK), lambda i, m: (0, 0, 0, chunk * ways + (m[0] ^ i)))
    whole = pl.BlockSpec((planes, slab, comps * BLOCK), lambda i, m: (0, 0, 0))
    got_spec, slots = markers_spec(got, slab)
    return pl.pallas_call(
        functools.partial(last_apart_body, comps, group, columns // BLOCK, chunk * ways, ways),
        out_shape=jax.ShapeDtypeStruct(field.shape, F32),
        grid_spec=pltpu.PrefetchScalarGridSpec(
            num_scalar_prefetch=1,
            grid=(ways,),
            in_specs=[
                pl.BlockSpec(order.shape, lambda i, m: (0, 0)),
                got_spec,
                pl.BlockSpec((planes, 1, slab, comps * BLOCK), lambda i, m: (0, 0, chunk, 0)),
            ]
            + [whole] * (ways - 1)
            + [spec]
            + [pl.BlockSpec(memory_space=pltpu.HBM)] * len(after),
            out_specs=spec,
            scratch_shapes=[
                pltpu.VMEM((slots, 4 * BLOCK), BF16),
                pltpu.VMEM((8, slots), jnp.int32),
                pltpu.VMEM((planes, slab, comps * BLOCK), BF16),
            ],
        ),
        input_output_aliases={4 + ways - 1: 0},
        compiler_params=pltpu.CompilerParams(vmem_limit_bytes=VMEM),
        cost_estimate=cost(LONG),
        name="last_apart",
    )(me, order, got, own, *pieces, field, *after)


def come_body(count, *refs):
    refs[count][...] = jnp.zeros_like(refs[count])


def come(pieces):
    return pl.pallas_call(
        functools.partial(come_body, len(pieces)),
        out_shape=jax.ShapeDtypeStruct((8, BLOCK), F32),
        in_specs=[pl.BlockSpec(memory_space=pltpu.HBM)] * len(pieces),
        out_specs=pl.BlockSpec(memory_space=pltpu.VMEM),
        cost_estimate=cost(LONG),
        name="come",
    )(*pieces)


def across(pieces):
    ways = lax.axis_size("col")
    return tuple(
        lax.ppermute(piece, "col", [(c, c ^ k) for c in range(ways)]) for k, piece in enumerate(pieces, 1)
    )


def along(x):
    return lax.all_to_all(x, "row", split_axis=0, concat_axis=0, tiled=True)


def exchange(x):
    return lax.all_to_all(x, AXES, split_axis=0, concat_axis=0, tiled=True)


def local(
    velocity,
    deriv_x,
    deriv_y,
    deriv_z,
    metric_x,
    metric_y,
    metric_z,
    ib_target,
    ib_owner,
    ib_block,
    ib_count,
):
    slab, planes, comps, columns = velocity.shape
    row_count, ways = lax.axis_size("row"), lax.axis_size("col")
    devices = row_count * ways
    groups = devices // planes
    group = min(32, slab)
    chunks = columns // (groups * BLOCK)
    me = lax.axis_index("col").astype(jnp.int32).reshape(1)
    lines = jnp.transpose(velocity, (0, 2, 1, 3)).reshape(slab * comps * planes, columns)
    order = jnp.asarray(pack_order(planes, comps, GROUP), BF16)
    quick = jnp.asarray(pack_order(planes, comps, GROUP // 2), BF16)
    back = jnp.asarray(unpack_order(planes, group), BF16)
    small = jnp.asarray(unpack_order(planes, LAST), BF16)
    metric_col = metric_z[:, None]
    apart = row_count == planes and chunks == QUARTERS and slab == QUARTERS * GROUP
    marked, *labels = markers(ib_target, ib_owner, ib_block, ib_count, me, devices, ways, apart)
    at_once = 2 if apart else chunks
    near_columns = columns // 2 if apart else 0
    first = pack(lines, quick, at_once, planes, comps, groups, slab)
    block = (devices,) + first.shape[2:]
    arrived = exchange(first.reshape(block)).reshape((row_count, ways) + first.shape[2:])
    *fields, far = near(
        lines, deriv_x, deriv_y, metric_x[None, :], metric_y[None, :], planes, comps, slab, near_columns, (first,)
    )

    if not apart:
        got = exchange(marked.reshape(devices, MOST, 4 * BLOCK))
        terms = depth(arrived, me, deriv_z, metric_col, at_once, slab, False, False, (far,))
        home = exchange(terms.reshape(block)).reshape(first.shape)
        far, weight = mark(far, got, columns, group, ())
        return jnp.transpose(last(None, far, weight, home, small), (0, 2, 1, 3))

    def outward(k, after, marked=None):
        return pack_apart(lines, order, me, k, planes, comps, ways, slab, after, marked)

    (field,) = fields
    marked = (marked.reshape(ways, planes, MOST, comps * BLOCK), labels[0].reshape(ways, planes, MOST, BLOCK))
    sent3 = outward(3, (field, metric_col))
    sent2 = outward(2, (sent3[0],), marked)
    later2, later3 = lax.optimization_barrier((sent2[EARLY:], sent3[EARLY:], arrived))[:2]
    come2 = across(tuple(sent2[1:EARLY]) + tuple(later2))
    come3 = across(tuple(sent3[1:EARLY]) + tuple(later3))
    terms = depth(arrived, me, deriv_z, metric_col, 2, slab, False, True, (sent2[0],))
    home = along(terms)
    joined2 = join((sent2[0],) + come2, (terms,))
    split0 = split(home, 0, slab, (joined2,))
    back0 = across(split0)
    split1 = split(home, 1, slab, (split0[0],))
    back1 = across(split1)
    got = full2 = along(joined2)
    joined3 = join((sent3[0],) + come3, (split1[0],))
    full3 = along(joined3)
    terms = depth(full2, me, deriv_z, metric_col, 1, slab, True, False, (joined3,), 0, 2)
    terms = depth(full3, me, deriv_z, metric_col, 1, slab, True, False, (come(back0),), 1, 2, (terms,))
    home_all = exchange(terms.reshape(block)).reshape(first.shape)
    field = last_apart(field, home, back0, got, back, me, 0, group, (terms,))
    field = last_apart(field, home, back1, got, back, me, 1, group, ())
    far, weight = mark(far, got, columns, group, (field,))
    return jnp.transpose(last(field, far, weight, home_all, small), (0, 2, 1, 3))


def solution(mesh):
    in_specs = (
        P(AXES, None, None, None),
        P(),
        P(),
        P(),
        P(),
        P(),
        P(),
        P(AXES, None, None, None),
        P(AXES, None),
        P(AXES, None),
        P(AXES),
    )
    out_specs = P(AXES, None, None, None)
    return jax.shard_map(local, mesh=mesh, in_specs=in_specs, out_specs=out_specs, check_vma=False)
```
